128 devices in a mesh: dp: 8 (over z_hi, x), space: 16 (over y, z_lo, core).
Axes of the slice: x: 4, y: 4, z: 4 (z_hi: 2, z_lo: 2; z = z_hi * 2 + z_lo), core: 2. Of those that a mesh axis runs over, the one named last changes fastest.
Arguments:
- volume: bfloat16 [8, 64, 32, 4096], P('dp', None, 'space'), may hold values from -6 to 6
- kernel_in: bfloat16 [1728, 128], replicated, may hold values from -0.15625 to 0.15625
- kernel_out: bfloat16 [3456, 128], P(None, 'space'), may hold values from -0.4375 to 0.4375
- cotangent: bfloat16 [8, 128, 16, 1024], P('dp', 'space'), may hold values from -24 to 24
Outputs:
- activation: bfloat16 [8, 128, 16, 1024], P('dp', 'space')
- volume_grad: bfloat16 [8, 64, 32, 4096], P('dp', None, 'space')
- first_grad: float32 [1728, 128], replicated
- second_grad: float32 [3456, 128], P(None, 'space')
The draws below stay inside these ranges and needn't reach their ends.
All inputs are finite; a program needn't handle non-finite values.
Results may differ from the reference program's by a relative error of at most 0.02.
Values may be sent and summed in bfloat16 or wider, within the bound.
No kernel may reach another device: no remote copies, remote signals or barrier semaphores. Data moves between devices by JAX's collectives and lax.ppermute only.
A program may use at most 128 MiB of HBM per device.

```python
import math
import jax
import jax.numpy as jnp
from jax import lax

C0 = 64
C1 = 128
C2 = 128
SIDE = 64
SAMPLES = 8
NZ = 32


def block_levels(rng, extent, cuts, smallest, largest):
    def one(axis_at, shards_of):
        heights = jax.random.uniform(jax.random.fold_in(jax.random.fold_in(rng, 6), axis_at), (shards_of,), jnp.float32, smallest / len(cuts), largest / len(cuts))
        return jnp.repeat(jnp.exp(heights), extent[axis_at] // shards_of).reshape((-1,) + (1,) * (len(extent) - axis_at - 1))

    level = one(*cuts[0])
    for cut in cuts[1:]:
        level = level * one(*cut)
    return level


def bell_draw(rng, shape, scale, bound, cuts=(), kind=jnp.bfloat16):
    gain = block_levels(rng, shape, cuts, -0.22, 0.18) if cuts else 1.0
    drawn = jax.random.normal(rng, shape, jnp.float32) * scale * gain
    return jnp.minimum(jnp.maximum(drawn, -bound), bound).astype(kind)


def setup_inputs(seed: int = 0) -> dict:
    splits = jax.random.split(jax.random.key(seed), 5)
    volume = bell_draw(splits[0], (SAMPLES, C0, NZ, SIDE * SIDE), 1.0, 6.0, ((0, 8), (2, 16)))
    kernel_in = bell_draw(splits[1], (27 * C0, C1), (27 * C0) ** -0.5, 0.15625)
    kernel_out = bell_draw(splits[2], (27 * C1, C2), (27 * C1 // 16) ** -0.5, 0.4375, ((1, 16),))
    cotangent = bell_draw(splits[3], (SAMPLES, C2, NZ // 2, SIDE * SIDE // 4), 4.0, 24.0, ((0, 8), (1, 16)))
    return {"volume": volume, "kernel_in": kernel_in, "kernel_out": kernel_out, "cotangent": cotangent}


LAYOUT = ('NCDHW', 'DHWIO', 'NCDHW')

def correlate(tensor, kernel):
    return lax.conv_general_dilated(tensor, kernel, (1, 1, 1), ((1, 1), (1, 1), (1, 1)), dimension_numbers=LAYOUT, precision=lax.Precision.HIGHEST)

def silu_slope(values):
    sigma = jax.nn.sigmoid(values)
    return sigma * (1.0 + values * (1.0 - sigma))

def average_pool(tensor):
    dims = tensor.shape
    return tensor.reshape(dims[0], dims[1], dims[2] // 2, 2, dims[3] // 2, 2, dims[4] // 2, 2).mean(axis=(3, 5, 7))

def spread_back(tensor):
    dims = tensor.shape
    wide = jnp.broadcast_to(tensor[:, :, :, None, :, None, :, None], (dims[0], dims[1], dims[2], 2, dims[3], 2, dims[4], 2))
    return wide.reshape(dims[0], dims[1], 2 * dims[2], 2 * dims[3], 2 * dims[4]) * 0.125

def reference(volume, kernel_in, kernel_out, cotangent):
    half_side = SIDE // 2
    kernel_first = kernel_in.astype(jnp.float32).reshape(3, 3, 3, C0, C1)
    kernel_second = kernel_out.astype(jnp.float32).reshape(3, 3, 3, C1, C2)

    def per_sample(item):
        sample, sample_cot = item
        sample_vol = sample.astype(jnp.float32).reshape(1, C0, NZ, SIDE, SIDE)
        pre_first = correlate(sample_vol, kernel_first)
        pooled = lax.optimization_barrier(average_pool(jax.nn.silu(pre_first)).astype(jnp.bfloat16)).astype(jnp.float32)
        pre_second = correlate(pooled, kernel_second)
        activation = jax.nn.silu(pre_second).astype(jnp.bfloat16)
        cot_field = sample_cot.astype(jnp.float32).reshape(1, C2, NZ // 2, half_side, half_side)
        slopes_second = lax.optimization_barrier((cot_field * silu_slope(pre_second)).astype(jnp.bfloat16)).astype(jnp.float32)
        unused_second, pull_second = jax.vjp(correlate, pooled, kernel_second)
        pooled_slope, second_term = pull_second(slopes_second)
        first_slopes = lax.optimization_barrier((spread_back(pooled_slope) * silu_slope(pre_first)).astype(jnp.bfloat16)).astype(jnp.float32)
        unused_first, pull_first = jax.vjp(correlate, sample_vol, kernel_first)
        volume_term, first_term = pull_first(first_slopes)
        return (activation.reshape(C2, NZ // 2, half_side * half_side), volume_term.astype(jnp.bfloat16).reshape(C0, NZ, SIDE * SIDE), first_term.reshape(27 * C0, C1), second_term.reshape(27 * C1, C2))
    activation, volume_grad, first_terms, second_terms = lax.map(per_sample, (volume, cotangent))
    cell_count = SAMPLES * NZ * SIDE * SIDE
    first_grad = lax.optimization_barrier(jnp.sum(first_terms, axis=0)) * (1.0 / math.sqrt(cell_count))
    second_grad = lax.optimization_barrier(jnp.sum(second_terms, axis=0)) * (1.0 / math.sqrt(cell_count // 8))
    return (activation, volume_grad, first_grad, second_grad)
```

```python
import math

import jax
import jax.numpy as jnp
from jax import lax
from jax.experimental import pallas as pl
from jax.experimental.pallas import tpu as pltpu
from jax.sharding import PartitionSpec as P

BF = jnp.bfloat16
F32 = jnp.float32
WINDOW = ((1, -1), (0, 0), (1, 0), (0, 1))
CELLS = 1024
NT = (((1,), (1,)), ((), ()))


def shape(dims, kind=BF):
    return jax.ShapeDtypeStruct(dims, kind)


def kernel_call(body, outs, *args, scratch=(), name):
    return pl.pallas_call(
        body,
        out_shape=outs,
        scratch_shapes=list(scratch),
        name=name,
        compiler_params=pltpu.CompilerParams(vmem_limit_bytes=60 << 20),
    )(*args)


def dot(a, b):
    return jnp.dot(a, b, preferred_element_type=F32)


def dot_nt(a, b):
    return lax.dot_general(a, b, NT, preferred_element_type=F32)


def sigmoid(v):
    return 1.0 / (1.0 + jnp.exp(-v))


def parity_matrix():
    row = lax.broadcasted_iota(jnp.int32, (512, 512), 0)
    col = lax.broadcasted_iota(jnp.int32, (512, 512), 1)
    phase = col // 128
    source = (2 * ((col % 128) // 32) + phase // 2) * 64 + 2 * (col % 32) + phase % 2
    return (row == source).astype(F32).astype(BF)


def shifted(x, oy, ox):
    step = (-(oy * 32 + ox)) % CELLS
    y = pltpu.roll(x, step, 1) if step else x
    if not (oy or ox):
        return y
    lane = lax.broadcasted_iota(jnp.int32, (1, CELLS), 1)
    keep = None
    if oy:
        keep = lane < CELLS - 32 if oy == 1 else lane >= 32
    if ox:
        inside = (lane % 32) != (31 if ox == 1 else 0)
        keep = inside if keep is None else keep & inside
    return jnp.where(keep, y, jnp.zeros((), x.dtype))


def fill_windows(parts, windows):
    for iy, (py, oy) in enumerate(WINDOW):
        for ix, (px, ox) in enumerate(WINDOW):
            at = (py * 2 + px) * CELLS
            row = 0
            for ref in parts:
                n = ref.shape[0]
                windows[iy * 4 + ix, row : row + n, :] = shifted(ref[:, at : at + CELLS], oy, ox)
                row += n


def split_body(vol, low, high, tmp):
    pm = parity_matrix()
    for b in range(8):
        y = dot(vol[0, :, :, b * 512 : (b + 1) * 512].reshape(128, 512), pm)
        t = tmp.at[b % 2]
        for p in range(4):
            t[p] = y[:, p * 128 : (p + 1) * 128]
        for z, out in ((0, low), (1, high)):
            for p in range(4):
                out[:, p * CELLS + b * 128 : p * CELLS + (b + 1) * 128] = t[
                    p, pl.ds(z, 64, stride=2), :
                ].astype(BF)


def first_weights_body(kin, forward, backward):
    zero = jnp.zeros((64, 128), BF)

    def block(dz, t):
        return kin[(dz * 9 + t) * 64 : (dz * 9 + t + 1) * 64, :] if 0 <= dz <= 2 else zero

    for t in range(9):
        rows = [jnp.concatenate([block(z, t), block(z - 1, t)], axis=1) for z in range(4)]
        both = jnp.concatenate(rows, axis=0)
        backward[:, (8 - t) * 256 : (9 - t) * 256] = both
        forward[:, t * 256 : (t + 1) * 256] = both.T


def send_body(cot, kout, out, tmp):
    for t in range(8):
        tmp[...] = cot[0, :, :, t * 128 : (t + 1) * 128].astype(F32).reshape(128, 128)
        for z in range(16):
            out[z, t * 8 : (t + 1) * 8, :] = tmp[pl.ds(z, 8, stride=16), :].astype(BF)
    for t in range(27):
        block = kout[t * 128 : (t + 1) * 128, :].astype(F32).T.astype(BF)
        for z in range(16):
            out[z, 64 + t * 8 : 72 + t * 8, :] = block


def tap_block(got, t):
    return got[:, 64 + t * 8 : 72 + t * 8, :].reshape(128, 128)


def second_weights_body(got, forward, backward):
    for t in range(27):
        z, y, x = t // 9, (t // 3) % 3, t % 3
        block = tap_block(got, t)
        forward[x * 128 : (x + 1) * 128, (z * 3 + y) * 128 : (z * 3 + y + 1) * 128] = block
        z, y, x = 2 - z, 2 - y, 2 - x
        backward[x * 128 : (x + 1) * 128, (z * 3 + y) * 128 : (z * 3 + y + 1) * 128] = block.T


def first_body(lo, low, high, hi, weights, pooled, slope, windows, total):
    fill_windows([lo, low, high, hi], windows)

    def phase(p, carry):
        py = p // 2
        px = p % 2
        for c in range(2):
            cols = slice(c * 512, (c + 1) * 512)
            v = None
            for dy in range(3):
                a = windows[pl.ds((py + dy) * 4 + px, 3), :, cols].reshape(768, 512)
                d = dot(weights[:, dy * 768 : (dy + 1) * 768], a)
                v = d if v is None else v + d
            s = sigmoid(v)
            slope[p, :, cols] = (s * (1.0 + v * (1.0 - s))).astype(BF)
            u = v * s
            u = u[:128] + u[128:]
            total[:, cols] = jnp.where(p == 0, 0.0, total[:, cols]) + u
        return carry

    total[...] = jnp.zeros_like(total)
    lax.fori_loop(0, 4, phase, 0)
    pooled[...] = (total[...] * 0.125).astype(BF)


def fill_rows(parts, rows):
    for z, ref in enumerate(parts):
        for y in range(3):
            at = (z * 3 + y) * 128
            rows[at : at + 128, :] = shifted(ref[...], y - 1, 0)


def folded(weights, rows):
    y = [dot(weights[x * 128 : (x + 1) * 128, :], rows[...]) for x in range(3)]
    return y[1] + shifted(y[0], 0, -1) + shifted(y[2], 0, 1)


def second_body(lo, own, hi, weights, got, act, slopes, rows):
    fill_rows([lo, own, hi], rows)
    v = folded(weights, rows)
    s = sigmoid(v)
    a = v * s
    g = s * (1.0 + v * (1.0 - s))
    for t in range(8):
        cols = slice(t * 128, (t + 1) * 128)
        cot = got[:, t * 8 : (t + 1) * 8, :].astype(F32).reshape(128, 128)
        slopes[:, cols] = (cot * g[:, cols]).astype(BF)
        act[:, t * 8 : (t + 1) * 8, :] = a[:, cols].reshape(16, 8, 128).astype(BF)


def second_grad_body(lo, own, hi, slopes, act, out, planes):
    for y in range(3):
        for x in range(3):
            for z, ref in enumerate((lo, own, hi)):
                planes[y * 3 + x, z * 128 : (z + 1) * 128, :] = shifted(ref[...], y - 1, x - 1)
    for t in range(9):
        g = dot_nt(slopes[...], planes[t])
        for z in range(3):
            at = 64 + (z * 9 + t) * 8
            out[:, at : at + 8, :] = g[:, z * 128 : (z + 1) * 128].reshape(16, 8, 128).astype(BF)
    out[:, 0:64, :] = act[...]


def first_grad_body(
    slo, own, shi, weights, slope, lo, low, high, hi, first_slopes, out, rows, windows, total
):
    fill_rows([slo, own, shi], rows)
    ps = folded(weights, rows) * 0.125
    for p in range(4):
        for z in range(2):
            first_slopes[z * 128 : (z + 1) * 128, p * CELLS : (p + 1) * CELLS] = (
                ps * slope[p, z * 128 : (z + 1) * 128, :].astype(F32)
            ).astype(BF)
    fill_windows([lo, low, high, hi], windows)
    for dy in range(3):
        for p in range(4):
            py, px = p // 2, p % 2
            a = windows[(py + dy) * 4 + px : (py + dy) * 4 + px + 3].reshape(768, CELLS)
            d = dot_nt(a, first_slopes[:, p * CELLS : (p + 1) * CELLS])
            if p == 0:
                total[...] = d
            else:
                total[...] += d
        for dx in range(3):
            for dz in range(3):
                t = dz * 9 + dy * 3 + dx
                at = dx * 256 + dz * 64
                out[t // 2, (t % 2) * 64 : (t % 2) * 64 + 64, :] = (
                    total[at : at + 64, 0:128] + total[at + 64 : at + 128, 128:256]
                ).astype(BF)
    zero = jnp.zeros((64, 128), BF)
    for t in range(27, 32):
        out[t // 2, (t % 2) * 64 : (t % 2) * 64 + 64, :] = zero


def volume_grad_body(first_slopes, weights, own, left, right, windows):
    fill_windows([first_slopes], windows)

    def phase(p, carry):
        py = p // 2
        px = p % 2
        for c in range(2):
            cols = slice(c * 512, (c + 1) * 512)
            v = None
            for dy in range(3):
                a = windows[pl.ds((py + dy) * 4 + px, 3), :, cols].reshape(768, 512)
                d = dot(weights[:, dy * 768 : (dy + 1) * 768], a)
                v = d if v is None else v + d
            at = pl.ds(pl.multiple_of(p * CELLS + c * 512, 512), 512)
            left[:, at] = v[0:64].astype(BF)
            own[:, at] = v[64:192]
            right[:, at] = v[192:256].astype(BF)
        return carry

    lax.fori_loop(0, 4, phase, 0)


def join_body(own, from_left, from_right, out, tmp):
    pm = parity_matrix()
    for b in range(8):
        pieces = []
        for p in range(4):
            at = slice(p * CELLS + b * 128, p * CELLS + (b + 1) * 128)
            first = own[0:64, at] + from_left[:, at].astype(F32)
            second = own[64:128, at] + from_right[:, at].astype(F32)
            pieces.append(jnp.concatenate([first, second], axis=0).astype(BF))
        y = dot_nt(jnp.concatenate(pieces, axis=1), pm)
        t = tmp.at[b % 2]
        for q in range(4):
            for z in range(2):
                t[q, pl.ds(z, 64, stride=2), :] = y[
                    z * 64 : (z + 1) * 64, q * 128 : (q + 1) * 128
                ]
        for q in range(4):
            at = slice(b * 512 + q * 128, b * 512 + (q + 1) * 128)
            out[0, :, :, at] = t[q].astype(BF).reshape(64, 2, 128)


def sum_second_body(got, out, act, tmp):
    for t in range(8):
        tmp[...] = got[:, t * 8 : (t + 1) * 8, :].astype(F32).reshape(128, 128)
        for o in range(8):
            act[0, o, :, t * 128 : (t + 1) * 128] = tmp[pl.ds(o, 16, stride=8), :].astype(BF)
    y = jnp.sum(got[:, 64:280, :].astype(F32), axis=0).astype(BF)
    for k in range(8):
        out[k] = y


def sum_first_body(got, out):
    y = jnp.sum(got[...].astype(F32), axis=0).astype(BF)
    for k in range(8):
        out[k] = y


def final_second_body(scale, got, out):
    y = jnp.sum(got[...].astype(F32), axis=0) * scale
    for t in range(27):
        out[t * 128 : (t + 1) * 128, :] = y[t * 8 : (t + 1) * 8, :].T


def final_first_body(scale, got, out):
    y = jnp.sum(got[...].astype(F32), axis=0) * scale
    for k in range(16):
        out[k] = y


def exchange(parts, axis):
    return lax.all_to_all(parts, axis, 0, 0, tiled=True)


def up(x):
    return lax.ppermute(x, "space", [(i, i + 1) for i in range(15)])


def down(x):
    return lax.ppermute(x, "space", [(i + 1, i) for i in range(15)])


def per_device(volume, kernel_in, kernel_out, cotangent):
    vm = pltpu.VMEM
    low, high = kernel_call(
        split_body, (shape((64, 4096)),) * 2, volume, scratch=[vm((2, 4, 128, 128), F32)],
        name="split",
    )
    lo, hi = up(high), down(low)
    packed = kernel_call(
        send_body, shape((16, 280, 128)), cotangent, kernel_out, scratch=[vm((128, 128), F32)],
        name="send",
    )
    got = exchange(packed, "space")
    w1, w1b = kernel_call(
        first_weights_body, (shape((256, 2304)),) * 2, kernel_in, name="first_weights"
    )
    pooled, slope = kernel_call(
        first_body, (shape((128, CELLS)), shape((4, 256, CELLS))), lo, low, high, hi, w1,
        scratch=[vm((16, 256, CELLS), BF), vm((128, CELLS), F32)], name="first",
    )
    plo, phi = up(pooled), down(pooled)
    w2, w2b = kernel_call(
        second_weights_body, (shape((384, 1152)),) * 2, got, name="second_weights"
    )
    act, slopes = kernel_call(
        second_body, (shape((16, 64, 128)), shape((128, CELLS))), plo, pooled, phi, w2, got,
        scratch=[vm((1152, CELLS), BF)], name="second",
    )
    slo, shi = up(slopes), down(slopes)
    packed = kernel_call(
        second_grad_body, shape((16, 280, 128)), plo, pooled, phi, slopes, act,
        scratch=[vm((9, 384, CELLS), BF)], name="second_grad",
    )
    got = exchange(packed, "space")
    first_slopes, packed = kernel_call(
        first_grad_body, (shape((256, 4096)), shape((16, 128, 128))),
        slo, slopes, shi, w2b, slope, lo, low, high, hi,
        scratch=[vm((1152, CELLS), BF), vm((16, 256, CELLS), BF), vm((768, 256), F32)],
        name="first_grad",
    )
    got_first = exchange(packed, "space")
    own, left, right = kernel_call(
        volume_grad_body, (shape((128, 4096), F32), shape((64, 4096)), shape((64, 4096))),
        first_slopes, w1b, scratch=[vm((16, 256, CELLS), BF)], name="volume_grad",
    )
    from_left, from_right = up(right), down(left)
    packed, activation = kernel_call(
        sum_second_body, (shape((8, 216, 128)), shape((1, 8, 16, CELLS))), got,
        scratch=[vm((128, 128), F32)], name="sum_second",
    )
    packed_first = kernel_call(sum_first_body, shape((8, 128, 128)), got_first, name="sum_first")
    got = exchange(jnp.concatenate([packed_first, packed], axis=1), "dp")
    volume_grad = kernel_call(
        join_body, shape((1, 64, 2, 4096)), own, from_left, from_right,
        scratch=[vm((2, 4, 128, 128), F32)], name="join",
    )
    cell_count = 8 * 32 * 4096
    first = kernel_call(
        lambda g, o: final_first_body(1.0 / math.sqrt(cell_count), g, o),
        shape((16, 128, 128), F32), got[:, :128], name="final_first",
    )
    first_grad = exchange(first, "space").reshape(2048, 128)[:1728]
    second_grad = kernel_call(
        lambda g, o: final_second_body(1.0 / math.sqrt(cell_count // 8), g, o),
        shape((3456, 8), F32), got[:, 128:], name="final_second",
    )
    return activation, volume_grad, first_grad, second_grad


def solution(mesh):
    return jax.shard_map(
        per_device,
        mesh=mesh,
        in_specs=(P("dp", None, "space", None), P(), P(None, "space"), P("dp", "space", None, None)),
        out_specs=(P("dp", "space", None, None), P("dp", None, "space", None), P(), P(None, "space")),
        check_vma=False,
    )
```

```python
import math

import jax
import jax.numpy as jnp
from jax import lax
from jax.experimental import pallas as pl
from jax.experimental.pallas import tpu as pltpu
from jax.sharding import Mesh
from jax.sharding import PartitionSpec as P


BF = jnp.bfloat16
F32 = jnp.float32
WINDOW = ((1, -1), (0, 0), (1, 0), (0, 1))
CELLS = 1024
NT = (((1,), (1,)), ((), ()))
SPACE = ("chip", "core")


def shape(dims, kind=BF):
    return jax.ShapeDtypeStruct(dims, kind)


def kernel_call(body, outs, *args, scratch=(), mib, hbm_in=(), hbm_out=(), scalar=()):
    def spec(k, far):
        if k in far:
            return pl.BlockSpec(memory_space=pltpu.HBM)
        return pl.BlockSpec()

    ins = [
        pl.BlockSpec(memory_space=pltpu.SMEM) if k in scalar else spec(k, hbm_in)
        for k in range(len(args))
    ]
    args = [
        pltpu.with_memory_space_constraint(x, pltpu.HBM) if k in hbm_in else x
        for k, x in enumerate(args)
    ]
    many = isinstance(outs, tuple)
    listed = outs if many else (outs,)
    out_specs = tuple(spec(k, hbm_out) for k in range(len(listed)))
    placed = tuple(
        pltpu.HBM(o.shape, o.dtype) if k in hbm_out else o for k, o in enumerate(listed)
    )
    return pl.pallas_call(
        body,
        out_shape=placed if many else placed[0],
        in_specs=ins,
        out_specs=out_specs if many else out_specs[0],
        scratch_shapes=list(scratch),
        compiler_params=pltpu.CompilerParams(vmem_limit_bytes=mib << 20),
    )(*args)


def dot(a, b):
    return jnp.dot(a, b, preferred_element_type=F32)


def dot_nt(a, b):
    return lax.dot_general(a, b, NT, preferred_element_type=F32)


def sigmoid(v):
    return 1.0 / (1.0 + jnp.exp(-v))


def parity_matrix():
    row = lax.broadcasted_iota(jnp.int32, (512, 512), 0)
    col = lax.broadcasted_iota(jnp.int32, (512, 512), 1)
    phase = col // 128
    source = (2 * ((col % 128) // 32) + phase // 2) * 64 + 2 * (col % 32) + phase % 2
    return (row == source).astype(F32).astype(BF)


def shifted(x, oy, ox):
    step = (-(oy * 32 + ox)) % CELLS
    y = pltpu.roll(x, step, 1) if step else x
    if not (oy or ox):
        return y
    lane = lax.broadcasted_iota(jnp.int32, (1, CELLS), 1)
    keep = None
    if oy:
        keep = lane < CELLS - 32 if oy == 1 else lane >= 32
    if ox:
        inside = (lane % 32) != (31 if ox == 1 else 0)
        keep = inside if keep is None else keep & inside
    return jnp.where(keep, y, jnp.zeros((), x.dtype))


def fill_windows(parts, windows):
    for iy, (py, oy) in enumerate(WINDOW):
        for ix, (px, ox) in enumerate(WINDOW):
            at = (py * 2 + px) * CELLS
            row = 0
            for ref in parts:
                n = ref.shape[0]
                windows[iy * 4 + ix, row : row + n, :] = shifted(ref[:, at : at + CELLS], oy, ox)
                row += n


def split_body(vol_in, low, high, tmp, vol, sems):
    copies = [
        pltpu.make_async_copy(vol_in.at[0, :, :, b * 512 : (b + 1) * 512], vol.at[b], sems.at[b])
        for b in range(8)
    ]
    for c in copies:
        c.start()
    pm = parity_matrix()
    for b in range(8):
        copies[b].wait()
        y = dot(vol[b].reshape(128, 512), pm)
        t = tmp.at[b % 2]
        for p in range(4):
            t[p] = y[:, p * 128 : (p + 1) * 128]
        for z, out in ((0, low), (1, high)):
            for p in range(4):
                out[:, p * CELLS + b * 128 : p * CELLS + (b + 1) * 128] = t[
                    p, pl.ds(z, 64, stride=2), :
                ].astype(BF)


def stacked_taps(kin, t):
    zero = jnp.zeros((64, 128), BF)

    def block(dz):
        return kin[(dz * 9 + t) * 64 : (dz * 9 + t + 1) * 64, :] if 0 <= dz <= 2 else zero

    rows = [jnp.concatenate([block(z), block(z - 1)], axis=1) for z in range(4)]
    return jnp.concatenate(rows, axis=0)


def first_weights_body(kin, forward):
    for t in range(9):
        forward[:, t * 256 : (t + 1) * 256] = stacked_taps(kin, t).T


def send_body(cot, kout_in, out, tmp, kout, sem):
    copy = pltpu.make_async_copy(kout_in, kout, sem)
    copy.start()
    for t in range(8):
        tmp[...] = cot[0, :, :, t * 128 : (t + 1) * 128].astype(F32).reshape(128, 128)
        for z in range(16):
            out[z, t * 8 : (t + 1) * 8, :] = tmp[pl.ds(z, 8, stride=16), :].astype(BF)
    copy.wait()
    for t in range(27):
        block = kout[:, t * 128 : (t + 1) * 128]
        for z in range(16):
            out[z, 64 + t * 8 : 72 + t * 8, :] = block


def tap_block(got, t):
    return got[:, 64 + t * 8 : 72 + t * 8, :].reshape(128, 128)


def fold_forward(got, forward):
    for t in range(27):
        z, y, x = t // 9, (t // 3) % 3, t % 3
        forward[x * 128 : (x + 1) * 128, (z * 3 + y) * 128 : (z * 3 + y + 1) * 128] = tap_block(got, t)


def fold_backward(got, backward):
    for t in range(27):
        z, y, x = 2 - t // 9, 2 - (t // 3) % 3, 2 - t % 3
        backward[x * 128 : (x + 1) * 128, (z * 3 + y) * 128 : (z * 3 + y + 1) * 128] = tap_block(got, t).T


def by_core(core, x):
    x = x.reshape(8, 2, *x.shape[1:])
    even, odd = x[:, 0], x[:, 1]
    return jnp.where(core == 0, even, odd), jnp.where(core == 0, odd, even)


def first_body(
    lo, low, high, hi, weights, pooled, slope_out, windows_out, windows, total, slope, sems
):
    fill_windows([lo, low, high, hi], windows)
    saved = pltpu.make_async_copy(windows, windows_out, sems.at[4])
    saved.start()

    def phase(p, carry):
        py = p // 2
        px = p % 2
        for c in range(2):
            cols = slice(c * 512, (c + 1) * 512)
            v = None
            for dy in range(3):
                a = windows[pl.ds((py + dy) * 4 + px, 3), :, cols].reshape(768, 512)
                d = dot(weights[:, dy * 768 : (dy + 1) * 768], a)
                v = d if v is None else v + d
            s = sigmoid(v)
            slope[p, :, cols] = (s * (1.0 + v * (1.0 - s))).astype(BF)
            u = v * s
            u = u[:128] + u[128:]
            total[:, cols] += u
        pltpu.make_async_copy(slope.at[p], slope_out.at[p], sems.at[p]).start()
        return carry

    total[...] = jnp.zeros_like(total)
    lax.fori_loop(0, 4, phase, 0)
    pooled[...] = (total[...] * 0.125).astype(BF)
    for p in range(4):
        pltpu.make_async_copy(slope.at[p], slope_out.at[p], sems.at[p]).wait()
    saved.wait()


def fill_rows(parts, rows):
    for z, ref in enumerate(parts):
        for y in range(3):
            at = (z * 3 + y) * 128
            rows[at : at + 128, :] = shifted(ref[...], y - 1, 0)


def folded(weights, rows):
    y = [dot(weights[x * 128 : (x + 1) * 128, :], rows[...]) for x in range(3)]
    return y[1] + shifted(y[0], 0, -1) + shifted(y[2], 0, 1)


def second_body(core, lo, own, hi, got, act_mine, act_other, slopes, rows, weights):
    fold_forward(got, weights)
    fill_rows([lo, own, hi], rows)
    v = folded(weights, rows)
    s = sigmoid(v)
    a = v * s
    g = s * (1.0 + v * (1.0 - s))
    for t in range(8):
        cols = slice(t * 128, (t + 1) * 128)
        cot = got[:, t * 8 : (t + 1) * 8, :].astype(F32).reshape(128, 128)
        slopes[:, cols] = (cot * g[:, cols]).astype(BF)
        mine, other = by_core(core[0], a[:, cols].reshape(16, 8, 128))
        act_mine[:, t * 8 : (t + 1) * 8, :] = mine.astype(BF)
        act_other[:, t * 8 : (t + 1) * 8, :] = other.astype(BF)


def second_grad_body(core, lo, own, hi, slopes, act_mine, act_other, out_mine, out_other, planes):
    for y in range(3):
        for x in range(3):
            for z, ref in enumerate((lo, own, hi)):
                planes[y * 3 + x, z * 128 : (z + 1) * 128, :] = shifted(ref[...], y - 1, x - 1)
    for t in range(9):
        g = dot_nt(slopes[...], planes[t])
        for z in range(3):
            at = 64 + (z * 9 + t) * 8
            mine, other = by_core(core[0], g[:, z * 128 : (z + 1) * 128].reshape(16, 8, 128))
            out_mine[:, at : at + 8, :] = mine.astype(BF)
            out_other[:, at : at + 8, :] = other.astype(BF)
    out_mine[:, 0:64, :] = act_mine[...]
    out_other[:, 0:64, :] = act_other[...]


def first_grad_body(
    core, slo, own, shi, got, slope_in, windows_in, first_slopes_out, out_mine, out_other, rows,
     windows, total, slope, weights, first_slopes, parts, sems,
):
    slope_copy = pltpu.make_async_copy(slope_in, slope, sems.at[4])
    slope_copy.start()
    loads = []
    for iy in range(4):
        at = pl.ds(iy * 4, 4)
        loads.append(pltpu.make_async_copy(windows_in.at[at], windows.at[at], sems.at[5 + iy]))
        loads[iy].start()
    fold_backward(got, weights)
    fill_rows([slo, own, shi], rows)
    ps = folded(weights, rows) * 0.125
    slope_copy.wait()
    for p in range(4):
        for z in range(2):
            first_slopes[p, z * 128 : (z + 1) * 128, :] = (
                ps * slope[p, z * 128 : (z + 1) * 128, :].astype(F32)
            ).astype(BF)
        pltpu.make_async_copy(first_slopes.at[p], first_slopes_out.at[p], sems.at[p]).start()
    for dy in range(3):
        for p in range(4):
            py, px = p // 2, p % 2
            if px == 0 and (py == 1 or dy == 0):
                loads[py + dy].wait()
            a = windows[(py + dy) * 4 + px : (py + dy) * 4 + px + 3].reshape(768, CELLS)
            d = dot_nt(a, first_slopes[p])
            if p == 0:
                total[...] = d
            else:
                total[...] += d
        for dx in range(3):
            for dz in range(3):
                t = dz * 9 + dy * 3 + dx
                at = dx * 256 + dz * 64
                side = jnp.where(core[0] == (t // 2) % 2, 0, 1)
                parts[side, t // 4, (t % 2) * 64 : (t % 2) * 64 + 64, :] = (
                    total[at : at + 64, 0:128] + total[at + 64 : at + 128, 128:256]
                ).astype(BF)
    for t in range(27, 32):
        side = jnp.where(core[0] == (t // 2) % 2, 0, 1)
        parts[side, t // 4, (t % 2) * 64 : (t % 2) * 64 + 64, :] = jnp.zeros((64, 128), BF)
    out_mine[...] = parts[0]
    out_other[...] = parts[1]
    for p in range(4):
        pltpu.make_async_copy(first_slopes.at[p], first_slopes_out.at[p], sems.at[p]).wait()


def pair_body(core, b_mine, b_other, a_mine, a_other, out):
    c = core[0] == 0
    out[:, 0:64, :] = jnp.where(c, b_mine[:, 0:64, :].astype(F32), b_other[:, 0:64, :].astype(F32)).astype(BF)
    out[:, 64:128, :] = jnp.where(c, b_other[:, 0:64, :].astype(F32), b_mine[:, 0:64, :].astype(F32)).astype(BF)
    out[:, 128:256, :] = (a_mine[...].astype(F32) + a_other[...].astype(F32)).astype(BF)
    out[:, 256:472, :] = (b_mine[:, 64:280, :].astype(F32) + b_other[:, 64:280, :].astype(F32)).astype(BF)


def volume_grad_body(
    slopes_in, kin_in, own_out, left, right, windows, slopes, kin, weights, own, sems
):
    copies = [pltpu.make_async_copy(slopes_in.at[p], slopes.at[p], sems.at[p]) for p in range(4)]
    copies.append(pltpu.make_async_copy(kin_in, kin, sems.at[4]))
    for c in copies:
        c.start()
    for p in range(4):
        copies[p].wait()
        for iy, (py, oy) in enumerate(WINDOW):
            for ix, (px, ox) in enumerate(WINDOW):
                if py * 2 + px == p:
                    windows[iy * 4 + ix] = shifted(slopes[p], oy, ox)
    copies[4].wait()
    for t in range(9):
        weights[:, (8 - t) * 256 : (9 - t) * 256] = stacked_taps(kin, t)

    def phase(p, carry):
        py = p // 2
        px = p % 2
        for c in range(2):
            cols = slice(c * 512, (c + 1) * 512)
            v = None
            for dy in range(3):
                a = windows[pl.ds((py + dy) * 4 + px, 3), :, cols].reshape(768, 512)
                d = dot(weights[:, dy * 768 : (dy + 1) * 768], a)
                v = d if v is None else v + d
            at = pl.ds(pl.multiple_of(p * CELLS + c * 512, 512), 512)
            left[:, at] = v[0:64].astype(BF)
            own[p, :, cols] = v[64:192]
            right[:, at] = v[192:256].astype(BF)
        pltpu.make_async_copy(own.at[p], own_out.at[p], sems.at[5 + p]).start()
        return carry

    lax.fori_loop(0, 4, phase, 0)
    for p in range(4):
        pltpu.make_async_copy(own.at[p], own_out.at[p], sems.at[5 + p]).wait()


def join_body(own_in, from_left, from_right, out, tmp, own, sems):
    copies = []
    for h in range(2):
        for p in range(4):
            at = slice(h * 512, (h + 1) * 512)
            copies.append(
                pltpu.make_async_copy(own_in.at[p, :, at], own.at[p, :, at], sems.at[h * 4 + p])
            )
    for c in copies:
        c.start()
    pm = parity_matrix()
    for b in range(8):
        if b % 4 == 0:
            for c in copies[b : b + 4]:
                c.wait()
        pieces = []
        for p in range(4):
            at = slice(p * CELLS + b * 128, p * CELLS + (b + 1) * 128)
            lanes = slice(b * 128, (b + 1) * 128)
            first = own[p, 0:64, lanes] + from_left[:, at].astype(F32)
            second = own[p, 64:128, lanes] + from_right[:, at].astype(F32)
            pieces.append(jnp.concatenate([first, second], axis=0).astype(BF))
        y = dot_nt(jnp.concatenate(pieces, axis=1), pm)
        t = tmp.at[b % 2]
        for q in range(4):
            for z in range(2):
                t[q, pl.ds(z, 64, stride=2), :] = y[
                    z * 64 : (z + 1) * 64, q * 128 : (q + 1) * 128
                ]
        for q in range(4):
            at = slice(b * 512 + q * 128, b * 512 + (q + 1) * 128)
            out[0, :, :, at] = t[q].astype(BF).reshape(64, 2, 128)


def merge_body(got, out):
    y = jnp.sum(got[:, 128:472, :].astype(F32), axis=0).astype(BF)
    for k in range(8):
        out[k] = y


def unpack_body(got, act, tmp):
    for t in range(8):
        for side in range(2):
            at = side * 64 + t * 8
            tmp[side] = got[:, at : at + 8, :].astype(F32).reshape(64, 128)
        for o in range(8):
            planes = [tmp[side, pl.ds(o, 8, stride=8), :].reshape(8, 1, 128) for side in range(2)]
            both = jnp.concatenate(planes, axis=1).reshape(16, 128)
            act[0, o, :, t * 128 : (t + 1) * 128] = both.astype(BF)


def final_second_body(scale, got, out):
    y = jnp.sum(got[:, 128:344, :].astype(F32), axis=0) * scale
    for t in range(27):
        out[:, t * 128 : (t + 1) * 128] = y[t * 8 : (t + 1) * 8, :]


def final_first_body(scale, got, out):
    y = (jnp.sum(got[:, 0:128, :].astype(F32), axis=0) * scale).astype(BF)
    for k in range(16):
        out[k] = y


def widen_body(got, out):
    for k in range(13):
        out[k * 128 : (k + 1) * 128, :] = got[k].astype(F32)
    out[13 * 128 : 1728, :] = got[13, 0:64, :].astype(F32)


def exchange(parts, axis):
    return lax.all_to_all(parts, axis, 0, 0, tiled=True)


def up(x):
    return lax.ppermute(x, SPACE, [(i, i + 1) for i in range(15)])


def down(x):
    return lax.ppermute(x, SPACE, [(i + 1, i) for i in range(15)])


def swap(x):
    return lax.ppermute(x, SPACE, [(i, i ^ 1) for i in range(16)])


def step(volume, kernel_in, kernel_out, cotangent):
    vm = pltpu.VMEM
    core = lax.axis_index("core").reshape(1)
    low, high = kernel_call(
        split_body, (shape((64, 4096)),) * 2, volume,
        scratch=[vm((2, 4, 128, 128), F32), vm((8, 64, 2, 512), BF), pltpu.SemaphoreType.DMA((8,))],
        mib=8, hbm_in=(0,),
    )
    lo, hi = up(high), down(low)
    packed = kernel_call(
        send_body, shape((16, 280, 128)), cotangent, kernel_out.T,
        scratch=[vm((128, 128), F32), vm((8, 3456), BF), pltpu.SemaphoreType.DMA(())],
        mib=8, hbm_in=(1,),
    )
    got = exchange(packed, SPACE)
    w1 = kernel_call(first_weights_body, shape((256, 2304)), kernel_in, mib=8)
    pooled, slope, windows = kernel_call(
        first_body,
        (shape((128, CELLS)), shape((4, 256, CELLS)), shape((16, 256, CELLS))), lo, low, high, hi, w1,
        scratch=[
            vm((16, 256, CELLS), BF), vm((128, CELLS), F32), vm((4, 256, CELLS), BF),
            pltpu.SemaphoreType.DMA((5,)),
        ],
        mib=20, hbm_out=(1, 2),
    )
    plo, phi = up(pooled), down(pooled)
    act_mine, act_other, slopes = kernel_call(
        second_body, (shape((8, 64, 128)), shape((8, 64, 128)), shape((128, CELLS))),
        core, plo, pooled, phi, got,
        scratch=[vm((1152, CELLS), BF), vm((384, 1152), BF)], mib=12, scalar=(0,),
    )
    slo, shi = up(slopes), down(slopes)
    b_mine, b_other = kernel_call(
        second_grad_body, (shape((8, 280, 128)),) * 2,
        core, plo, pooled, phi, slopes, act_mine, act_other,
        scratch=[vm((9, 384, CELLS), BF)], mib=14, scalar=(0,),
    )
    b_other = swap(b_other)
    first_slopes, a_mine, a_other = kernel_call(
        first_grad_body,
        (shape((4, 256, CELLS)), shape((8, 128, 128)), shape((8, 128, 128))),
        core, slo, slopes, shi, got, slope, windows,
        scratch=[
            vm((1152, CELLS), BF), vm((16, 256, CELLS), BF), vm((768, 256), F32),
            vm((4, 256, CELLS), BF), vm((384, 1152), BF), vm((4, 256, CELLS), BF),
            vm((2, 8, 128, 128), BF), pltpu.SemaphoreType.DMA((9,)),
        ],
        mib=28, scalar=(0,), hbm_in=(5, 6), hbm_out=(0,),
    )
    a_other = swap(a_other)
    packed = kernel_call(
        pair_body, shape((8, 472, 128)), core, b_mine, b_other, a_mine, a_other,
        mib=8, scalar=(0,),
    )
    got = exchange(packed, "chip")
    own, left, right = kernel_call(
        volume_grad_body, (shape((4, 128, CELLS), F32), shape((64, 4096)), shape((64, 4096))),
        first_slopes, kernel_in,
        scratch=[
            vm((16, 256, CELLS), BF), vm((4, 256, CELLS), BF), vm((1728, 128), BF),
            vm((256, 2304), BF), vm((4, 128, CELLS), F32), pltpu.SemaphoreType.DMA((9,)),
        ],
        mib=24, hbm_in=(0, 1), hbm_out=(0,),
    )
    packed = kernel_call(merge_body, shape((8, 344, 128)), got, mib=8)
    summed = exchange(packed, "dp")
    from_left, from_right = up(right), down(left)
    activation = kernel_call(
        unpack_body, shape((1, 8, 16, CELLS)), got, scratch=[vm((2, 64, 128), F32)],
        mib=8,
    )
    cell_count = 8 * 32 * 4096
    packed = kernel_call(
        lambda g, o: final_first_body(1.0 / math.sqrt(cell_count), g, o),
        shape((16, 128, 128)), summed, mib=8,
    )
    got = exchange(packed, SPACE)
    volume_grad = kernel_call(
        join_body, shape((1, 64, 2, 4096)), own, from_left, from_right,
        scratch=[vm((2, 4, 128, 128), F32), vm((4, 128, CELLS), F32), pltpu.SemaphoreType.DMA((8,))],
        mib=12, hbm_in=(0,),
    )
    second_grad = kernel_call(
        lambda g, o: final_second_body(1.0 / math.sqrt(cell_count // 8), g, o),
        shape((8, 3456), F32), summed, mib=8,
    ).T
    first_grad = kernel_call(widen_body, shape((1728, 128), F32), got, mib=8)
    return activation, volume_grad, first_grad, second_grad


def solution(mesh):
    finer = Mesh(mesh.devices.reshape(mesh.shape["dp"], 8, 2), ("dp", "chip", "core"))
    return jax.shard_map(
        step,
        mesh=finer,
        in_specs=(P("dp", None, SPACE, None), P(), P(None, SPACE), P("dp", SPACE, None, None)),
        out_specs=(P("dp", SPACE, None, None), P("dp", None, SPACE, None), P(), P(None, SPACE)),
        check_vma=False,
    )
```

```python
import math

import jax
import jax.numpy as jnp
from jax import lax
from jax.experimental import pallas as pl
from jax.experimental.pallas import tpu as pltpu
from jax.sharding import Mesh
from jax.sharding import PartitionSpec as P


BF = jnp.bfloat16
F32 = jnp.float32
WINDOW = ((1, -1), (0, 0), (1, 0), (0, 1))
CELLS = 1024
NT = (((1,), (1,)), ((), ()))
SPACE = ("chip", "core")


def shape(dims, kind=BF):
    return jax.ShapeDtypeStruct(dims, kind)


def kernel_call(body, outs, *args, scratch=(), mib, hbm_in=(), hbm_out=(), scalar=()):
    def spec(k, far):
        if k in far:
            return pl.BlockSpec(memory_space=pltpu.HBM)
        return pl.BlockSpec()

    ins = [
        pl.BlockSpec(memory_space=pltpu.SMEM) if k in scalar else spec(k, hbm_in)
        for k in range(len(args))
    ]
    args = [
        pltpu.with_memory_space_constraint(x, pltpu.HBM) if k in hbm_in else x
        for k, x in enumerate(args)
    ]
    many = isinstance(outs, tuple)
    listed = outs if many else (outs,)
    out_specs = tuple(spec(k, hbm_out) for k in range(len(listed)))
    placed = tuple(
        pltpu.HBM(o.shape, o.dtype) if k in hbm_out else o for k, o in enumerate(listed)
    )
    return pl.pallas_call(
        body,
        out_shape=placed if many else placed[0],
        in_specs=ins,
        out_specs=out_specs if many else out_specs[0],
        scratch_shapes=list(scratch),
        compiler_params=pltpu.CompilerParams(vmem_limit_bytes=mib << 20),
    )(*args)


def dot(a, b):
    return jnp.dot(a, b, preferred_element_type=F32)


def dot_nt(a, b):
    return lax.dot_general(a, b, NT, preferred_element_type=F32)


def sigmoid(v):
    return 1.0 / (1.0 + jnp.exp(-v))


def parity_matrix():
    row = lax.broadcasted_iota(jnp.int32, (512, 512), 0)
    col = lax.broadcasted_iota(jnp.int32, (512, 512), 1)
    phase = col // 128
    source = (2 * ((col % 128) // 32) + phase // 2) * 64 + 2 * (col % 32) + phase % 2
    return (row == source).astype(F32).astype(BF)


def shifted(x, oy, ox):
    step = (-(oy * 32 + ox)) % CELLS
    y = pltpu.roll(x, step, 1) if step else x
    if not (oy or ox):
        return y
    lane = lax.broadcasted_iota(jnp.int32, (1, CELLS), 1)
    keep = None
    if oy:
        keep = lane < CELLS - 32 if oy == 1 else lane >= 32
    if ox:
        inside = (lane % 32) != (31 if ox == 1 else 0)
        keep = inside if keep is None else keep & inside
    return jnp.where(keep, y, jnp.zeros((), x.dtype))


def fill_windows(parts, windows):
    for iy, (py, oy) in enumerate(WINDOW):
        for ix, (px, ox) in enumerate(WINDOW):
            at = (py * 2 + px) * CELLS
            row = 0
            for ref in parts:
                n = ref.shape[0]
                windows[iy * 4 + ix, row : row + n, :] = shifted(ref[:, at : at + CELLS], oy, ox)
                row += n


def split_body(vol, low, high, tmp):
    pm = parity_matrix()
    for b in range(8):
        y = dot(vol[0, :, :, b * 512 : (b + 1) * 512].reshape(128, 512), pm)
        t = tmp.at[b % 2]
        for p in range(4):
            t[p] = y[:, p * 128 : (p + 1) * 128]
        for z, out in ((0, low), (1, high)):
            for p in range(4):
                out[:, p * CELLS + b * 128 : p * CELLS + (b + 1) * 128] = t[
                    p, pl.ds(z, 64, stride=2), :
                ].astype(BF)


def stacked_taps(kin, t):
    zero = jnp.zeros((64, 128), BF)

    def block(dz):
        return kin[(dz * 9 + t) * 64 : (dz * 9 + t + 1) * 64, :] if 0 <= dz <= 2 else zero

    rows = [jnp.concatenate([block(z), block(z - 1)], axis=1) for z in range(4)]
    return jnp.concatenate(rows, axis=0)


def first_weights_body(kin, forward):
    for t in range(9):
        forward[:, t * 256 : (t + 1) * 256] = stacked_taps(kin, t).T


def send_body(cot_in, kout_in, out, tmp, cot, kout, sems):
    copies = [
        pltpu.make_async_copy(cot_in, cot, sems.at[0]),
        pltpu.make_async_copy(kout_in, kout, sems.at[1]),
    ]
    for c in copies:
        c.start()
    copies[0].wait()
    for t in range(8):
        tmp[...] = cot[0, :, :, t * 128 : (t + 1) * 128].astype(F32).reshape(128, 128)
        for z in range(16):
            at = (z % 2) * 280 + t * 8
            out[z // 2, at : at + 8, :] = tmp[pl.ds(z, 8, stride=16), :].astype(BF)
    copies[1].wait()
    for t in range(27):
        block = kout[:, t * 128 : (t + 1) * 128]
        for q in range(8):
            out[q, 64 + t * 8 : 72 + t * 8, :] = block


def all_channels(got, at):
    return jnp.stack([got[0, :, at, :], got[1, :, at, :]], axis=1).reshape(128, 128)


def fold_taps(got, forward, backward):
    for t in range(27):
        z, y, x = t // 9, (t // 3) % 3, t % 3
        block = all_channels(got, slice(64 + t * 8, 72 + t * 8))
        forward[x * 128 : (x + 1) * 128, (z * 3 + y) * 128 : (z * 3 + y + 1) * 128] = block
        z, y, x = 2 - z, 2 - y, 2 - x
        backward[x * 128 : (x + 1) * 128, (z * 3 + y) * 128 : (z * 3 + y + 1) * 128] = block.T


def by_core(core, x):
    x = x.reshape(8, 2, *x.shape[1:])
    even, odd = x[:, 0], x[:, 1]
    return jnp.where(core == 0, even, odd), jnp.where(core == 0, odd, even)


def first_body(
    lo, low, high, hi, weights, pooled, slope_out, planes_out, windows, total, slope, sems
):
    saved = [
        pltpu.make_async_copy(r, planes_out.at[k], sems.at[4 + k])
        for k, r in enumerate((lo, low, high, hi))
    ]
    for c in saved:
        c.start()
    fill_windows([lo, low, high, hi], windows)

    def phase(p, carry):
        py = p // 2
        px = p % 2
        for c in range(2):
            cols = slice(c * 512, (c + 1) * 512)
            v = None
            for dy in range(3):
                a = windows[pl.ds((py + dy) * 4 + px, 3), :, cols].reshape(768, 512)
                d = dot(weights[:, dy * 768 : (dy + 1) * 768], a)
                v = d if v is None else v + d
            s = sigmoid(v)
            slope[p, :, cols] = (s * (1.0 + v * (1.0 - s))).astype(BF)
            u = v * s
            u = u[:128] + u[128:]
            total[:, cols] += u
        pltpu.make_async_copy(slope.at[p], slope_out.at[p], sems.at[p]).start()
        return carry

    total[...] = jnp.zeros_like(total)
    lax.fori_loop(0, 4, phase, 0)
    pooled[...] = (total[...] * 0.125).astype(BF)
    for p in range(4):
        pltpu.make_async_copy(slope.at[p], slope_out.at[p], sems.at[p]).wait()
    for c in saved:
        c.wait()


def fill_rows(parts, rows):
    for z, ref in enumerate(parts):
        for y in range(3):
            at = (z * 3 + y) * 128
            rows[at : at + 128, :] = shifted(ref[...], y - 1, 0)


def folded(weights, rows):
    y = [dot(weights[x * 128 : (x + 1) * 128, :], rows[...]) for x in range(3)]
    return y[1] + shifted(y[0], 0, -1) + shifted(y[2], 0, 1)


def second_body(
    core, lo, own, hi, got_mine, got_other, act_mine, act_other, slopes, backward, rows, weights,
    got, sems,
):
    copies = [
        pltpu.make_async_copy(got_mine, got.at[core[0]], sems.at[0]),
        pltpu.make_async_copy(got_other, got.at[1 - core[0]], sems.at[1]),
    ]
    for c in copies:
        c.start()
    fill_rows([lo, own, hi], rows)
    for c in copies:
        c.wait()
    fold_taps(got, weights, backward)
    first_row = pl.multiple_of(core[0] * 280, 8)
    v = folded(weights, rows)
    s = sigmoid(v)
    a = v * s
    g = s * (1.0 + v * (1.0 - s))
    for t in range(8):
        cols = slice(t * 128, (t + 1) * 128)
        cot = all_channels(got, pl.ds(first_row + t * 8, 8)).astype(F32)
        slopes[:, cols] = (cot * g[:, cols]).astype(BF)
        mine, other = by_core(core[0], a[:, cols].reshape(16, 8, 128))
        act_mine[:, t * 8 : (t + 1) * 8, :] = mine.astype(BF)
        act_other[:, t * 8 : (t + 1) * 8, :] = other.astype(BF)


def second_grad_body(core, lo, own, hi, slopes, act_mine, act_other, out_mine, out_other, planes):
    for y in range(3):
        for x in range(3):
            for z, ref in enumerate((lo, own, hi)):
                planes[y * 3 + x, z * 128 : (z + 1) * 128, :] = shifted(ref[...], y - 1, x - 1)
    for t in range(9):
        g = dot_nt(slopes[...], planes[t])
        for z in range(3):
            at = 64 + (z * 9 + t) * 8
            mine, other = by_core(core[0], g[:, z * 128 : (z + 1) * 128].reshape(16, 8, 128))
            out_mine[:, at : at + 8, :] = mine.astype(BF)
            out_other[:, at : at + 8, :] = other.astype(BF)
    out_mine[:, 0:64, :] = act_mine[...]
    out_other[:, 0:64, :] = act_other[...]


def share_of(row):
    return row // 112, row % 112


def put(core, parts, row, values):
    done = 0
    while done < 64:
        share, at = share_of(row + done)
        n = min(64 - done, 112 - at)
        side = jnp.where(core[0] == share % 2, 0, 1)
        parts[side, share // 2, at : at + n, :] = values[done : done + n].astype(BF)
        done += n


def first_grad_body(
    core, slo, own, shi, weights, slope_in, planes_in, first_slopes_out, out_mine, out_other, rows,
    windows, total, slope, planes, first_slopes, parts, sems,
):
    planes_copy = pltpu.make_async_copy(planes_in, planes, sems.at[5])
    planes_copy.start()
    slope_copy = pltpu.make_async_copy(slope_in, slope, sems.at[4])
    slope_copy.start()
    fill_rows([slo, own, shi], rows)
    ps = folded(weights, rows) * 0.125
    slope_copy.wait()
    for p in range(4):
        for z in range(2):
            first_slopes[p, z * 128 : (z + 1) * 128, :] = (
                ps * slope[p, z * 128 : (z + 1) * 128, :].astype(F32)
            ).astype(BF)
        pltpu.make_async_copy(first_slopes.at[p], first_slopes_out.at[p], sems.at[p]).start()
    planes_copy.wait()
    fill_windows([planes.at[k] for k in range(4)], windows)
    for dy in range(3):
        for p in range(4):
            py, px = p // 2, p % 2
            a = windows[(py + dy) * 4 + px : (py + dy) * 4 + px + 3].reshape(768, CELLS)
            d = dot_nt(a, first_slopes[p])
            if p == 0:
                total[...] = d
            else:
                total[...] += d
        for dx in range(3):
            for dz in range(3):
                t = dz * 9 + dy * 3 + dx
                at = dx * 256 + dz * 64
                g = total[at : at + 64, 0:128] + total[at + 64 : at + 128, 128:256]
                put(core, parts, t * 64, g)
    put(core, parts, 1728, jnp.zeros((64, 128), F32))
    out_mine[...] = parts[0]
    out_other[...] = parts[1]
    for p in range(4):
        pltpu.make_async_copy(first_slopes.at[p], first_slopes_out.at[p], sems.at[p]).wait()


def pair_body(core, b_mine, b_other, a_mine, a_other, out):
    c = core[0] == 0
    out[:, 0:64, :] = jnp.where(c, b_mine[:, 0:64, :].astype(F32), b_other[:, 0:64, :].astype(F32)).astype(BF)
    out[:, 64:128, :] = jnp.where(c, b_other[:, 0:64, :].astype(F32), b_mine[:, 0:64, :].astype(F32)).astype(BF)
    out[:, 128:240, :] = (a_mine[...].astype(F32) + a_other[...].astype(F32)).astype(BF)
    out[:, 240:456, :] = (b_mine[:, 64:280, :].astype(F32) + b_other[:, 64:280, :].astype(F32)).astype(BF)


def volume_grad_body(
    slopes_in, kin_in, own_out, left, right, windows, slopes, kin, weights, own, sems
):
    copies = [pltpu.make_async_copy(slopes_in.at[p], slopes.at[p], sems.at[p]) for p in range(4)]
    copies.append(pltpu.make_async_copy(kin_in, kin, sems.at[4]))
    for c in copies:
        c.start()
    for p in range(4):
        copies[p].wait()
        for iy, (py, oy) in enumerate(WINDOW):
            for ix, (px, ox) in enumerate(WINDOW):
                if py * 2 + px == p:
                    windows[iy * 4 + ix] = shifted(slopes[p], oy, ox)
    copies[4].wait()
    for t in range(9):
        weights[:, (8 - t) * 256 : (9 - t) * 256] = stacked_taps(kin, t)

    def phase(p, carry):
        py = p // 2
        px = p % 2
        for c in range(2):
            cols = slice(c * 512, (c + 1) * 512)
            v = None
            for dy in range(3):
                a = windows[pl.ds((py + dy) * 4 + px, 3), :, cols].reshape(768, 512)
                d = dot(weights[:, dy * 768 : (dy + 1) * 768], a)
                v = d if v is None else v + d
            at = pl.ds(pl.multiple_of(p * CELLS + c * 512, 512), 512)
            left[:, at] = v[0:64].astype(BF)
            own[p, :, cols] = v[64:192]
            right[:, at] = v[192:256].astype(BF)
        pltpu.make_async_copy(own.at[p], own_out.at[p], sems.at[5 + p]).start()
        return carry

    lax.fori_loop(0, 4, phase, 0)
    for p in range(4):
        pltpu.make_async_copy(own.at[p], own_out.at[p], sems.at[5 + p]).wait()


def join_body(own_in, from_left, from_right, out, tmp, own, sems):
    copies = []
    for h in range(2):
        for p in range(4):
            at = slice(h * 512, (h + 1) * 512)
            copies.append(
                pltpu.make_async_copy(own_in.at[p, :, at], own.at[p, :, at], sems.at[h * 4 + p])
            )
    for c in copies:
        c.start()
    pm = parity_matrix()
    for b in range(8):
        if b % 4 == 0:
            for c in copies[b : b + 4]:
                c.wait()
        pieces = []
        for p in range(4):
            at = slice(p * CELLS + b * 128, p * CELLS + (b + 1) * 128)
            lanes = slice(b * 128, (b + 1) * 128)
            first = own[p, 0:64, lanes] + from_left[:, at].astype(F32)
            second = own[p, 64:128, lanes] + from_right[:, at].astype(F32)
            pieces.append(jnp.concatenate([first, second], axis=0).astype(BF))
        y = dot_nt(jnp.concatenate(pieces, axis=1), pm)
        t = tmp.at[b % 2]
        for q in range(4):
            for z in range(2):
                t[q, pl.ds(z, 64, stride=2), :] = y[
                    z * 64 : (z + 1) * 64, q * 128 : (q + 1) * 128
                ]
        for q in range(4):
            at = slice(b * 512 + q * 128, b * 512 + (q + 1) * 128)
            out[0, :, :, at] = t[q].astype(BF).reshape(64, 2, 128)


def merge_body(got, out):
    y = jnp.sum(got[:, 128:456, :].astype(F32), axis=0).astype(BF)
    for k in range(8):
        out[k] = y


def unpack_body(got, act, tmp):
    for t in range(8):
        for side in range(2):
            at = side * 64 + t * 8
            tmp[side] = got[:, at : at + 8, :].astype(F32).reshape(64, 128)
        for o in range(8):
            planes = [tmp[side, pl.ds(o, 8, stride=8), :].reshape(8, 1, 128) for side in range(2)]
            both = jnp.concatenate(planes, axis=1).reshape(16, 128)
            act[0, o, :, t * 128 : (t + 1) * 128] = both.astype(BF)


def final_second_body(scale, got, out):
    y = jnp.sum(got[:, 112:328, :].astype(F32), axis=0) * scale
    for t in range(27):
        out[:, t * 128 : (t + 1) * 128] = y[t * 8 : (t + 1) * 8, :]


def final_first_body(scale, got, out):
    y = (jnp.sum(got[:, 0:112, :].astype(F32), axis=0) * scale).astype(BF)
    for k in range(16):
        out[k] = y


def widen_body(got, out):
    for k in range(16):
        n = min(112, 1728 - k * 112)
        out[k * 112 : k * 112 + n, :] = got[k, 0:n, :].astype(F32)


def exchange(parts, axis):
    return lax.all_to_all(parts, axis, 0, 0, tiled=True)


def up(x):
    return lax.ppermute(x, SPACE, [(i, i + 1) for i in range(15)])


def down(x):
    return lax.ppermute(x, SPACE, [(i + 1, i) for i in range(15)])


def swap(x):
    return lax.ppermute(x, SPACE, [(i, i ^ 1) for i in range(16)])


def step(volume, kernel_in, kernel_out, cotangent):
    vm = pltpu.VMEM
    core = lax.axis_index("core").reshape(1)
    low, high = kernel_call(
        split_body, (shape((64, 4096)),) * 2, volume,
        scratch=[vm((2, 4, 128, 128), F32)], mib=8,
    )
    lo, hi = up(high), down(low)
    packed = kernel_call(
        send_body, shape((8, 344, 128)), cotangent, kernel_out.T,
        scratch=[
            vm((128, 128), F32), vm((1, 8, 16, CELLS), BF), vm((8, 3456), BF),
            pltpu.SemaphoreType.DMA((2,)),
        ],
        mib=8, hbm_in=(0, 1),
    )
    got_mine = exchange(packed, "chip")
    got_other = swap(got_mine)
    w1 = kernel_call(first_weights_body, shape((256, 2304)), kernel_in, mib=8)
    pooled, slope, planes = kernel_call(
        first_body,
        (shape((128, CELLS)), shape((4, 256, CELLS)), shape((4, 64, 4096))), lo, low, high, hi, w1,
        scratch=[
            vm((16, 256, CELLS), BF), vm((128, CELLS), F32), vm((4, 256, CELLS), BF),
            pltpu.SemaphoreType.DMA((8,)),
        ],
        mib=20, hbm_out=(1, 2),
    )
    plo, phi = up(pooled), down(pooled)
    act_mine, act_other, slopes, w2b = kernel_call(
        second_body,
        (shape((8, 64, 128)), shape((8, 64, 128)), shape((128, CELLS)), shape((384, 1152))),
        core, plo, pooled, phi, got_mine, got_other,
        scratch=[
            vm((1152, CELLS), BF), vm((384, 1152), BF), vm((2, 8, 344, 128), BF),
            pltpu.SemaphoreType.DMA((2,)),
        ],
        mib=14, scalar=(0,),
    )
    slo, shi = up(slopes), down(slopes)
    b_mine, b_other = kernel_call(
        second_grad_body, (shape((8, 280, 128)),) * 2,
        core, plo, pooled, phi, slopes, act_mine, act_other,
        scratch=[vm((9, 384, CELLS), BF)], mib=14, scalar=(0,),
    )
    b_other = swap(b_other)
    first_slopes, a_mine, a_other = kernel_call(
        first_grad_body,
        (shape((4, 256, CELLS)), shape((8, 112, 128)), shape((8, 112, 128))),
        core, slo, slopes, shi, w2b, slope, planes,
        scratch=[
            vm((1152, CELLS), BF), vm((16, 256, CELLS), BF), vm((768, 256), F32),
            vm((4, 256, CELLS), BF), vm((4, 64, 4096), BF), vm((4, 256, CELLS), BF),
            vm((2, 8, 112, 128), BF), pltpu.SemaphoreType.DMA((6,)),
        ],
        mib=28, scalar=(0,), hbm_in=(5, 6), hbm_out=(0,),
    )
    a_other = swap(a_other)
    packed = kernel_call(
        pair_body, shape((8, 456, 128)), core, b_mine, b_other, a_mine, a_other,
        mib=8, scalar=(0,),
    )
    got = exchange(packed, "chip")
    own, left, right = kernel_call(
        volume_grad_body, (shape((4, 128, CELLS), F32), shape((64, 4096)), shape((64, 4096))),
        first_slopes, kernel_in,
        scratch=[
            vm((16, 256, CELLS), BF), vm((4, 256, CELLS), BF), vm((1728, 128), BF),
            vm((256, 2304), BF), vm((4, 128, CELLS), F32), pltpu.SemaphoreType.DMA((9,)),
        ],
        mib=24, hbm_in=(0, 1), hbm_out=(0,),
    )
    packed = kernel_call(merge_body, shape((8, 328, 128)), got, mib=8)
    summed = exchange(packed, "dp")
    from_left, from_right = up(right), down(left)
    activation = kernel_call(
        unpack_body, shape((1, 8, 16, CELLS)), got, scratch=[vm((2, 64, 128), F32)],
        mib=8,
    )
    cell_count = 8 * 32 * 4096
    packed = kernel_call(
        lambda g, o: final_first_body(1.0 / math.sqrt(cell_count), g, o),
        shape((16, 112, 128)), summed, mib=8,
    )
    got = exchange(packed, SPACE)
    volume_grad = kernel_call(
        join_body, shape((1, 64, 2, 4096)), own, from_left, from_right,
        scratch=[vm((2, 4, 128, 128), F32), vm((4, 128, CELLS), F32), pltpu.SemaphoreType.DMA((8,))],
        mib=12, hbm_in=(0,),
    )
    second_grad = kernel_call(
        lambda g, o: final_second_body(1.0 / math.sqrt(cell_count // 8), g, o),
        shape((8, 3456), F32), summed, mib=8,
    ).T
    first_grad = kernel_call(widen_body, shape((1728, 128), F32), got, mib=8)
    return activation, volume_grad, first_grad, second_grad


def solution(mesh):
    finer = Mesh(mesh.devices.reshape(mesh.shape["dp"], 8, 2), ("dp", "chip", "core"))
    return jax.shard_map(
        step,
        mesh=finer,
        in_specs=(P("dp", None, SPACE, None), P(), P(None, SPACE), P("dp", SPACE, None, None)),
        out_specs=(P("dp", SPACE, None, None), P("dp", None, SPACE, None), P(), P(None, SPACE)),
        check_vma=False,
    )
```

```python
import math

import jax
import jax.numpy as jnp
from jax import lax
from jax.experimental import pallas as pl
from jax.experimental.pallas import tpu as pltpu
from jax.sharding import Mesh
from jax.sharding import PartitionSpec as P


BF = jnp.bfloat16
F32 = jnp.float32
WINDOW = ((1, -1), (0, 0), (1, 0), (0, 1))
CELLS = 1024
NT = (((1,), (1,)), ((), ()))
DP = ("zh", "x")
SPACE = ("chip", "core")


def shape(dims, kind=BF):
    return jax.ShapeDtypeStruct(dims, kind)


def kernel_call(body, outs, *args, scratch=(), mib, hbm_in=(), hbm_out=(), scalar=()):
    def spec(k, far):
        if k in far:
            return pl.BlockSpec(memory_space=pltpu.HBM)
        return pl.BlockSpec()

    ins = [
        pl.BlockSpec(memory_space=pltpu.SMEM) if k in scalar else spec(k, hbm_in)
        for k in range(len(args))
    ]
    args = [
        pltpu.with_memory_space_constraint(x, pltpu.HBM) if k in hbm_in else x
        for k, x in enumerate(args)
    ]
    many = isinstance(outs, tuple)
    listed = outs if many else (outs,)
    out_specs = tuple(spec(k, hbm_out) for k in range(len(listed)))
    placed = tuple(
        pltpu.HBM(o.shape, o.dtype) if k in hbm_out else o for k, o in enumerate(listed)
    )
    return pl.pallas_call(
        body,
        out_shape=placed if many else placed[0],
        in_specs=ins,
        out_specs=out_specs if many else out_specs[0],
        scratch_shapes=list(scratch),
        compiler_params=pltpu.CompilerParams(vmem_limit_bytes=mib << 20),
    )(*args)


def dot(a, b):
    return jnp.dot(a, b, preferred_element_type=F32)


def dot_nt(a, b):
    return lax.dot_general(a, b, NT, preferred_element_type=F32)


def sigmoid(v):
    return 1.0 / (1.0 + jnp.exp(-v))


def parity_matrix():
    row = lax.broadcasted_iota(jnp.int32, (512, 512), 0)
    col = lax.broadcasted_iota(jnp.int32, (512, 512), 1)
    phase = col // 128
    source = (2 * ((col % 128) // 32) + phase // 2) * 64 + 2 * (col % 32) + phase % 2
    return (row == source).astype(F32).astype(BF)


def shifted(x, oy, ox):
    step = (-(oy * 32 + ox)) % CELLS
    y = pltpu.roll(x, step, 1) if step else x
    if not (oy or ox):
        return y
    lane = lax.broadcasted_iota(jnp.int32, (1, CELLS), 1)
    keep = None
    if oy:
        keep = lane < CELLS - 32 if oy == 1 else lane >= 32
    if ox:
        inside = (lane % 32) != (31 if ox == 1 else 0)
        keep = inside if keep is None else keep & inside
    return jnp.where(keep, y, jnp.zeros((), x.dtype))


def fill_windows(parts, windows):
    for iy, (py, oy) in enumerate(WINDOW):
        for ix, (px, ox) in enumerate(WINDOW):
            at = (py * 2 + px) * CELLS
            row = 0
            for ref in parts:
                n = ref.shape[0]
                windows[iy * 4 + ix, row : row + n, :] = shifted(ref[:, at : at + CELLS], oy, ox)
                row += n


def split_body(vol, low, high, tmp):
    pm = parity_matrix()
    for b in range(8):
        y = dot(vol[0, :, :, b * 512 : (b + 1) * 512].reshape(128, 512), pm)
        t = tmp.at[b % 2]
        for p in range(4):
            t[p] = y[:, p * 128 : (p + 1) * 128]
        for z, out in ((0, low), (1, high)):
            for p in range(4):
                out[:, p * CELLS + b * 128 : p * CELLS + (b + 1) * 128] = t[
                    p, pl.ds(z, 64, stride=2), :
                ].astype(BF)


def stacked_taps(kin, t):
    zero = jnp.zeros((64, 128), BF)

    def block(dz):
        return kin[(dz * 9 + t) * 64 : (dz * 9 + t + 1) * 64, :] if 0 <= dz <= 2 else zero

    rows = [jnp.concatenate([block(z), block(z - 1)], axis=1) for z in range(4)]
    return jnp.concatenate(rows, axis=0)


def first_weights_body(kin, forward):
    for t in range(9):
        forward[:, t * 256 : (t + 1) * 256] = stacked_taps(kin, t).T


def send_body(cot_in, kout_in, out, tmp, cot, kout, sems):
    copies = [
        pltpu.make_async_copy(cot_in, cot, sems.at[0]),
        pltpu.make_async_copy(kout_in, kout, sems.at[1]),
    ]
    for c in copies:
        c.start()
    copies[0].wait()
    for t in range(8):
        tmp[t % 2] = cot[0, :, :, t * 128 : (t + 1) * 128].astype(F32).reshape(128, 128)
        for z in range(16):
            out[z, t * 8 : (t + 1) * 8, :] = tmp[t % 2, pl.ds(z, 8, stride=16), :].astype(BF)
    copies[1].wait()
    for t in range(27):
        block = kout[:, t * 128 : (t + 1) * 128]
        for z in range(16):
            out[z, 64 + t * 8 : 72 + t * 8, :] = block


def all_channels(got, at):
    return got[:, at, :].reshape(128, 128)


def fold_taps(got, forward, backward):
    for t in range(27):
        z, y, x = t // 9, (t // 3) % 3, t % 3
        block = all_channels(got, slice(64 + t * 8, 72 + t * 8))
        forward[x * 128 : (x + 1) * 128, (z * 3 + y) * 128 : (z * 3 + y + 1) * 128] = block
        z, y, x = 2 - z, 2 - y, 2 - x
        backward[x * 128 : (x + 1) * 128, (z * 3 + y) * 128 : (z * 3 + y + 1) * 128] = block.T


def by_core(core, x):
    x = x.reshape(8, 2, *x.shape[1:])
    even, odd = x[:, 0], x[:, 1]
    return jnp.where(core == 0, even, odd), jnp.where(core == 0, odd, even)


def first_body(
    lo, low, high, hi, weights, pooled, slope_out, planes_out, windows, total, slope, sems
):
    saved = [
        pltpu.make_async_copy(r, planes_out.at[k], sems.at[4 + k])
        for k, r in enumerate((lo, low, high, hi))
    ]
    for c in saved:
        c.start()
    fill_windows([lo, low, high, hi], windows)

    def phase(p, carry):
        py = p // 2
        px = p % 2
        for c in range(2):
            cols = slice(c * 512, (c + 1) * 512)
            v = None
            for dy in range(3):
                a = windows[pl.ds((py + dy) * 4 + px, 3), :, cols].reshape(768, 512)
                d = dot(weights[:, dy * 768 : (dy + 1) * 768], a)
                v = d if v is None else v + d
            s = sigmoid(v)
            slope[p, :, cols] = (s * (1.0 + v * (1.0 - s))).astype(BF)
            u = v * s
            u = u[:128] + u[128:]
            total[:, cols] += u
        pltpu.make_async_copy(slope.at[p], slope_out.at[p], sems.at[p]).start()
        return carry

    total[...] = jnp.zeros_like(total)
    lax.fori_loop(0, 4, phase, 0)
    pooled[...] = (total[...] * 0.125).astype(BF)
    for p in range(4):
        pltpu.make_async_copy(slope.at[p], slope_out.at[p], sems.at[p]).wait()
    for c in saved:
        c.wait()


def fill_rows(parts, rows):
    for z, ref in enumerate(parts):
        for y in range(3):
            at = (z * 3 + y) * 128
            rows[at : at + 128, :] = shifted(ref[...], y - 1, 0)


def folded(weights, rows):
    y = [dot(weights[x * 128 : (x + 1) * 128, :], rows[...]) for x in range(3)]
    return y[1] + shifted(y[0], 0, -1) + shifted(y[2], 0, 1)


def second_body(
    core, lo, own, hi, got, act_mine, act_other, slopes, backward, rows, weights
):
    fold_taps(got, weights, backward)
    fill_rows([lo, own, hi], rows)
    v = folded(weights, rows)
    s = sigmoid(v)
    a = v * s
    g = s * (1.0 + v * (1.0 - s))
    for t in range(8):
        cols = slice(t * 128, (t + 1) * 128)
        cot = all_channels(got, slice(t * 8, (t + 1) * 8)).astype(F32)
        slopes[:, cols] = (cot * g[:, cols]).astype(BF)
        mine, other = by_core(core[0], a[:, cols].reshape(16, 8, 128))
        act_mine[:, t * 8 : (t + 1) * 8, :] = mine.astype(BF)
        act_other[:, t * 8 : (t + 1) * 8, :] = other.astype(BF)


def second_grad_body(core, lo, own, hi, slopes, act_mine, act_other, out_mine, out_other, planes):
    for y in range(3):
        for x in range(3):
            for z, ref in enumerate((lo, own, hi)):
                planes[y * 3 + x, z * 128 : (z + 1) * 128, :] = shifted(ref[...], y - 1, x - 1)
    for t in range(9):
        g = dot_nt(slopes[...], planes[t])
        for z in range(3):
            at = 64 + (z * 9 + t) * 8
            mine, other = by_core(core[0], g[:, z * 128 : (z + 1) * 128].reshape(16, 8, 128))
            out_mine[:, at : at + 8, :] = mine.astype(BF)
            out_other[:, at : at + 8, :] = other.astype(BF)
    out_mine[:, 0:64, :] = act_mine[...]
    out_other[:, 0:64, :] = act_other[...]


def share_of(row):
    return row // 112, row % 112


def put(core, parts, row, values):
    done = 0
    while done < 64:
        share, at = share_of(row + done)
        n = min(64 - done, 112 - at)
        side = jnp.where(core[0] == share % 2, 0, 1)
        parts[side, share // 2, at : at + n, :] = values[done : done + n].astype(BF)
        done += n


def first_grad_body(
    core, slo, own, shi, weights, slope_in, planes_in, first_slopes_out, out_mine, out_other, rows,
    windows, total, slope, planes, first_slopes, parts, sems,
):
    planes_copy = pltpu.make_async_copy(planes_in, planes, sems.at[5])
    planes_copy.start()
    slope_copy = pltpu.make_async_copy(slope_in, slope, sems.at[4])
    slope_copy.start()
    fill_rows([slo, own, shi], rows)
    ps = folded(weights, rows) * 0.125
    slope_copy.wait()
    for p in range(4):
        for z in range(2):
            first_slopes[p, z * 128 : (z + 1) * 128, :] = (
                ps * slope[p, z * 128 : (z + 1) * 128, :].astype(F32)
            ).astype(BF)
        pltpu.make_async_copy(first_slopes.at[p], first_slopes_out.at[p], sems.at[p]).start()
    planes_copy.wait()
    fill_windows([planes.at[k] for k in range(4)], windows)
    for dy in range(3):
        for p in range(4):
            py, px = p // 2, p % 2
            a = windows[(py + dy) * 4 + px : (py + dy) * 4 + px + 3].reshape(768, CELLS)
            d = dot_nt(a, first_slopes[p])
            if p == 0:
                total[...] = d
            else:
                total[...] += d
        for dx in range(3):
            for dz in range(3):
                t = dz * 9 + dy * 3 + dx
                at = dx * 256 + dz * 64
                g = total[at : at + 64, 0:128] + total[at + 64 : at + 128, 128:256]
                put(core, parts, t * 64, g)
    put(core, parts, 1728, jnp.zeros((64, 128), F32))
    out_mine[...] = parts[0]
    out_other[...] = parts[1]
    for p in range(4):
        pltpu.make_async_copy(first_slopes.at[p], first_slopes_out.at[p], sems.at[p]).wait()


def pair_body(core, b_mine, b_other, a_mine, a_other, out):
    c = core[0] == 0
    out[:, 0:64, :] = jnp.where(c, b_mine[:, 0:64, :].astype(F32), b_other[:, 0:64, :].astype(F32)).astype(BF)
    out[:, 64:128, :] = jnp.where(c, b_other[:, 0:64, :].astype(F32), b_mine[:, 0:64, :].astype(F32)).astype(BF)
    out[:, 128:240, :] = (a_mine[...].astype(F32) + a_other[...].astype(F32)).astype(BF)
    out[:, 240:456, :] = (b_mine[:, 64:280, :].astype(F32) + b_other[:, 64:280, :].astype(F32)).astype(BF)


def volume_grad_body(
    slopes_in, kin_in, own_out, left, right, windows, slopes, kin, weights, own, sems
):
    copies = [pltpu.make_async_copy(slopes_in.at[p], slopes.at[p], sems.at[p]) for p in range(4)]
    copies.append(pltpu.make_async_copy(kin_in, kin, sems.at[4]))
    for c in copies:
        c.start()
    for p in range(4):
        copies[p].wait()
        for iy, (py, oy) in enumerate(WINDOW):
            for ix, (px, ox) in enumerate(WINDOW):
                if py * 2 + px == p:
                    windows[iy * 4 + ix] = shifted(slopes[p], oy, ox)
    copies[4].wait()
    for t in range(9):
        weights[:, (8 - t) * 256 : (9 - t) * 256] = stacked_taps(kin, t)

    def phase(p, carry):
        py = p // 2
        px = p % 2
        for c in range(2):
            cols = slice(c * 512, (c + 1) * 512)
            v = None
            for dy in range(3):
                a = windows[pl.ds((py + dy) * 4 + px, 3), :, cols].reshape(768, 512)
                d = dot(weights[:, dy * 768 : (dy + 1) * 768], a)
                v = d if v is None else v + d
            at = pl.ds(pl.multiple_of(p * CELLS + c * 512, 512), 512)
            left[:, at] = v[0:64].astype(BF)
            own[p, :, cols] = v[64:192]
            right[:, at] = v[192:256].astype(BF)
        pltpu.make_async_copy(own.at[p], own_out.at[p], sems.at[5 + p]).start()
        return carry

    lax.fori_loop(0, 4, phase, 0)
    for p in range(4):
        pltpu.make_async_copy(own.at[p], own_out.at[p], sems.at[5 + p]).wait()


def join_body(own_in, from_left, from_right, out, tmp, own, sems):
    copies = []
    for h in range(2):
        for p in range(4):
            at = slice(h * 512, (h + 1) * 512)
            copies.append(
                pltpu.make_async_copy(own_in.at[p, :, at], own.at[p, :, at], sems.at[h * 4 + p])
            )
    for c in copies:
        c.start()
    pm = parity_matrix()
    for b in range(8):
        if b % 4 == 0:
            for c in copies[b : b + 4]:
                c.wait()
        pieces = []
        for p in range(4):
            at = slice(p * CELLS + b * 128, p * CELLS + (b + 1) * 128)
            lanes = slice(b * 128, (b + 1) * 128)
            first = own[p, 0:64, lanes] + from_left[:, at].astype(F32)
            second = own[p, 64:128, lanes] + from_right[:, at].astype(F32)
            pieces.append(jnp.concatenate([first, second], axis=0).astype(BF))
        y = dot_nt(jnp.concatenate(pieces, axis=1), pm)
        t = tmp.at[b % 2]
        for q in range(4):
            for z in range(2):
                t[q, pl.ds(z, 64, stride=2), :] = y[
                    z * 64 : (z + 1) * 64, q * 128 : (q + 1) * 128
                ]
        for q in range(4):
            at = slice(b * 512 + q * 128, b * 512 + (q + 1) * 128)
            out[0, :, :, at] = t[q].astype(BF).reshape(64, 2, 128)


def merge_body(got, out):
    y = jnp.sum(got[:, 128:456, :].astype(F32), axis=0).astype(BF)
    for k in range(4):
        out[k] = y


def row_sum_body(got, out):
    out[...] = jnp.sum(got[...].astype(F32), axis=0).astype(BF)


def unpack_body(got, act, tmp):
    for t in range(8):
        for side in range(2):
            at = side * 64 + t * 8
            tmp[side] = got[:, at : at + 8, :].astype(F32).reshape(64, 128)
        for o in range(8):
            planes = [tmp[side, pl.ds(o, 8, stride=8), :].reshape(8, 1, 128) for side in range(2)]
            both = jnp.concatenate(planes, axis=1).reshape(16, 128)
            act[0, o, :, t * 128 : (t + 1) * 128] = both.astype(BF)


def final_second_body(scale, a, b, out):
    y = (a[112:328, :].astype(F32) + b[112:328, :].astype(F32)) * scale
    for t in range(27):
        out[:, t * 128 : (t + 1) * 128] = y[t * 8 : (t + 1) * 8, :]


def final_first_body(scale, a, b, out):
    y = ((a[0:112, :].astype(F32) + b[0:112, :].astype(F32)) * scale).astype(BF)
    for k in range(16):
        out[k] = y


def widen_body(got, out):
    for k in range(16):
        n = min(112, 1728 - k * 112)
        out[k * 112 : k * 112 + n, :] = got[k, 0:n, :].astype(F32)


def exchange(parts, axis):
    return lax.all_to_all(parts, axis, 0, 0, tiled=True)


def up(x):
    return lax.ppermute(x, SPACE, [(i, i + 1) for i in range(15)])


def down(x):
    return lax.ppermute(x, SPACE, [(i + 1, i) for i in range(15)])


def swap(x):
    return lax.ppermute(x, SPACE, [(i, i ^ 1) for i in range(16)])


def step(volume, kernel_in, kernel_out, cotangent):
    vm = pltpu.VMEM
    core = lax.axis_index("core").reshape(1)
    low, high = kernel_call(
        split_body, (shape((64, 4096)),) * 2, volume,
        scratch=[vm((2, 4, 128, 128), F32)], mib=8,
    )
    lo, hi = up(high), down(low)
    packed = kernel_call(
        send_body, shape((16, 280, 128)), cotangent, kernel_out.T,
        scratch=[
            vm((2, 128, 128), F32), vm((1, 8, 16, CELLS), BF), vm((8, 3456), BF),
            pltpu.SemaphoreType.DMA((2,)),
        ],
        mib=8, hbm_in=(0, 1),
    )
    got = exchange(packed, SPACE)
    w1 = kernel_call(first_weights_body, shape((256, 2304)), kernel_in, mib=8)
    pooled, slope, planes = kernel_call(
        first_body,
        (shape((128, CELLS)), shape((4, 256, CELLS)), shape((4, 64, 4096))), lo, low, high, hi, w1,
        scratch=[
            vm((16, 256, CELLS), BF), vm((128, CELLS), F32), vm((4, 256, CELLS), BF),
            pltpu.SemaphoreType.DMA((8,)),
        ],
        mib=20, hbm_out=(1, 2),
    )
    plo, phi = up(pooled), down(pooled)
    act_mine, act_other, slopes, w2b = kernel_call(
        second_body,
        (shape((8, 64, 128)), shape((8, 64, 128)), shape((128, CELLS)), shape((384, 1152))),
        core, plo, pooled, phi, got, scratch=[vm((1152, CELLS), BF), vm((384, 1152), BF)],
        mib=14, scalar=(0,),
    )
    slo, shi = up(slopes), down(slopes)
    b_mine, b_other = kernel_call(
        second_grad_body, (shape((8, 280, 128)),) * 2,
        core, plo, pooled, phi, slopes, act_mine, act_other,
        scratch=[vm((9, 384, CELLS), BF)], mib=14, scalar=(0,),
    )
    b_other = swap(b_other)
    first_slopes, a_mine, a_other = kernel_call(
        first_grad_body,
        (shape((4, 256, CELLS)), shape((8, 112, 128)), shape((8, 112, 128))),
        core, slo, slopes, shi, w2b, slope, planes,
        scratch=[
            vm((1152, CELLS), BF), vm((16, 256, CELLS), BF), vm((768, 256), F32),
            vm((4, 256, CELLS), BF), vm((4, 64, 4096), BF), vm((4, 256, CELLS), BF),
            vm((2, 8, 112, 128), BF), pltpu.SemaphoreType.DMA((6,)),
        ],
        mib=28, scalar=(0,), hbm_in=(5, 6), hbm_out=(0,),
    )
    a_other = swap(a_other)
    packed = kernel_call(
        pair_body, shape((8, 456, 128)), core, b_mine, b_other, a_mine, a_other,
        mib=8, scalar=(0,),
    )
    got = exchange(packed, "chip")
    own, left, right = kernel_call(
        volume_grad_body, (shape((4, 128, CELLS), F32), shape((64, 4096)), shape((64, 4096))),
        first_slopes, kernel_in,
        scratch=[
            vm((16, 256, CELLS), BF), vm((4, 256, CELLS), BF), vm((1728, 128), BF),
            vm((256, 2304), BF), vm((4, 128, CELLS), F32), pltpu.SemaphoreType.DMA((9,)),
        ],
        mib=24, hbm_in=(0, 1), hbm_out=(0,),
    )
    from_left, from_right = up(right), down(left)
    packed = kernel_call(merge_body, shape((4, 328, 128)), got, mib=8)
    rows = exchange(packed, "x")
    row = kernel_call(row_sum_body, shape((328, 128)), rows, mib=8)
    row_far = lax.ppermute(row, "zh", [(0, 1), (1, 0)])
    activation = kernel_call(
        unpack_body, shape((1, 8, 16, CELLS)), got, scratch=[vm((2, 64, 128), F32)],
        mib=8,
    )
    cell_count = 8 * 32 * 4096
    packed = kernel_call(
        lambda a, b, o: final_first_body(1.0 / math.sqrt(cell_count), a, b, o),
        shape((16, 112, 128)), row, row_far, mib=8,
    )
    got = exchange(packed, SPACE)
    volume_grad = kernel_call(
        join_body, shape((1, 64, 2, 4096)), own, from_left, from_right,
        scratch=[vm((2, 4, 128, 128), F32), vm((4, 128, CELLS), F32), pltpu.SemaphoreType.DMA((8,))],
        mib=12, hbm_in=(0,),
    )
    second_grad = kernel_call(
        lambda a, b, o: final_second_body(1.0 / math.sqrt(cell_count // 8), a, b, o),
        shape((8, 3456), F32), row, row_far, mib=8,
    ).T
    first_grad = kernel_call(widen_body, shape((1728, 128), F32), got, mib=8)
    return activation, volume_grad, first_grad, second_grad


def solution(mesh):
    finer = Mesh(mesh.devices.reshape(2, 4, 8, 2), ("zh", "x", "chip", "core"))
    return jax.shard_map(
        step,
        mesh=finer,
        in_specs=(P(DP, None, SPACE, None), P(), P(None, SPACE), P(DP, SPACE, None, None)),
        out_specs=(P(DP, SPACE, None, None), P(DP, None, SPACE, None), P(), P(None, SPACE)),
        check_vma=False,
    )
```

```python
import math

import jax
import jax.numpy as jnp
from jax import lax
from jax.experimental import pallas as pl
from jax.experimental.pallas import tpu as pltpu
from jax.sharding import Mesh
from jax.sharding import PartitionSpec as P


BF = jnp.bfloat16
F32 = jnp.float32
WINDOW = ((1, -1), (0, 0), (1, 0), (0, 1))
CELLS = 1024
NT = (((1,), (1,)), ((), ()))
DP = ("zh", "x")
SPACE = ("chip", "core")


def shape(dims, kind=BF):
    return jax.ShapeDtypeStruct(dims, kind)


def kernel_call(body, outs, *args, scratch=(), mib, hbm_in=(), hbm_out=(), scalar=()):
    def spec(k, far):
        if k in far:
            return pl.BlockSpec(memory_space=pltpu.HBM)
        return pl.BlockSpec()

    ins = [
        pl.BlockSpec(memory_space=pltpu.SMEM) if k in scalar else spec(k, hbm_in)
        for k in range(len(args))
    ]
    args = [
        pltpu.with_memory_space_constraint(x, pltpu.HBM) if k in hbm_in else x
        for k, x in enumerate(args)
    ]
    many = isinstance(outs, tuple)
    listed = outs if many else (outs,)
    out_specs = tuple(spec(k, hbm_out) for k in range(len(listed)))
    placed = tuple(
        pltpu.HBM(o.shape, o.dtype) if k in hbm_out else o for k, o in enumerate(listed)
    )
    return pl.pallas_call(
        body,
        out_shape=placed if many else placed[0],
        in_specs=ins,
        out_specs=out_specs if many else out_specs[0],
        scratch_shapes=list(scratch),
        compiler_params=pltpu.CompilerParams(vmem_limit_bytes=mib << 20),
    )(*args)


def dot(a, b):
    return jnp.dot(a, b, preferred_element_type=F32)


def dot_nt(a, b):
    return lax.dot_general(a, b, NT, preferred_element_type=F32)


def sigmoid(v):
    return 1.0 / (1.0 + jnp.exp(-v))


def parity_matrix():
    row = lax.broadcasted_iota(jnp.int32, (512, 512), 0)
    col = lax.broadcasted_iota(jnp.int32, (512, 512), 1)
    phase = col // 128
    source = (2 * ((col % 128) // 32) + phase // 2) * 64 + 2 * (col % 32) + phase % 2
    return (row == source).astype(F32).astype(BF)


def shifted(x, oy, ox):
    step = (-(oy * 32 + ox)) % CELLS
    y = pltpu.roll(x, step, 1) if step else x
    if not (oy or ox):
        return y
    lane = lax.broadcasted_iota(jnp.int32, (1, CELLS), 1)
    keep = None
    if oy:
        keep = lane < CELLS - 32 if oy == 1 else lane >= 32
    if ox:
        inside = (lane % 32) != (31 if ox == 1 else 0)
        keep = inside if keep is None else keep & inside
    return jnp.where(keep, y, jnp.zeros((), x.dtype))


def fill_windows(parts, windows):
    for iy, (py, oy) in enumerate(WINDOW):
        for ix, (px, ox) in enumerate(WINDOW):
            at = (py * 2 + px) * CELLS
            row = 0
            for ref in parts:
                n = ref.shape[0]
                windows[iy * 4 + ix, row : row + n, :] = shifted(ref[:, at : at + CELLS], oy, ox)
                row += n


def split_body(vol, low, high, tmp):
    pm = parity_matrix()
    for b in range(8):
        y = dot(vol[0, :, :, b * 512 : (b + 1) * 512].reshape(128, 512), pm)
        t = tmp.at[b % 2]
        for p in range(4):
            t[p] = y[:, p * 128 : (p + 1) * 128]
        for z, out in ((0, low), (1, high)):
            for p in range(4):
                out[:, p * CELLS + b * 128 : p * CELLS + (b + 1) * 128] = t[
                    p, pl.ds(z, 64, stride=2), :
                ].astype(BF)


def stacked_taps(kin, t):
    zero = jnp.zeros((64, 128), BF)

    def block(dz):
        return kin[(dz * 9 + t) * 64 : (dz * 9 + t + 1) * 64, :] if 0 <= dz <= 2 else zero

    rows = [jnp.concatenate([block(z), block(z - 1)], axis=1) for z in range(4)]
    return jnp.concatenate(rows, axis=0)


def first_weights_body(kin, forward):
    for t in range(9):
        forward[:, t * 256 : (t + 1) * 256] = stacked_taps(kin, t).T


def send_body(cot_in, kout_in, out, tmp, cot, kout, sems):
    copies = [
        pltpu.make_async_copy(cot_in, cot, sems.at[0]),
        pltpu.make_async_copy(kout_in, kout, sems.at[1]),
    ]
    for c in copies:
        c.start()
    copies[0].wait()
    for t in range(8):
        tmp[t % 2] = cot[0, :, :, t * 128 : (t + 1) * 128].astype(F32).reshape(128, 128)
        for z in range(16):
            out[z, t * 8 : (t + 1) * 8, :] = tmp[t % 2, pl.ds(z, 8, stride=16), :].astype(BF)
    copies[1].wait()
    for t in range(27):
        block = kout[:, t * 128 : (t + 1) * 128]
        for z in range(16):
            out[z, 64 + t * 8 : 72 + t * 8, :] = block


def all_channels(got, at):
    return got[:, at, :].reshape(128, 128)


def fold_taps(got, forward, backward):
    for t in range(27):
        z, y, x = t // 9, (t // 3) % 3, t % 3
        block = all_channels(got, slice(64 + t * 8, 72 + t * 8))
        forward[x * 128 : (x + 1) * 128, (z * 3 + y) * 128 : (z * 3 + y + 1) * 128] = block
        z, y, x = 2 - z, 2 - y, 2 - x
        backward[x * 128 : (x + 1) * 128, (z * 3 + y) * 128 : (z * 3 + y + 1) * 128] = block.T


def by_core(core, x):
    x = x.reshape(8, 2, *x.shape[1:])
    even, odd = x[:, 0], x[:, 1]
    return jnp.where(core == 0, even, odd), jnp.where(core == 0, odd, even)


def first_body(
    lo, low, high, hi, weights, pooled, slope_out, planes_out, windows, total, slope, sems
):
    saved = [
        pltpu.make_async_copy(r, planes_out.at[k], sems.at[4 + k])
        for k, r in enumerate((lo, low, high, hi))
    ]
    for c in saved:
        c.start()
    fill_windows([lo, low, high, hi], windows)

    def phase(p, carry):
        py = p // 2
        px = p % 2
        for c in range(2):
            cols = slice(c * 512, (c + 1) * 512)
            v = None
            for dy in range(3):
                a = windows[pl.ds((py + dy) * 4 + px, 3), :, cols].reshape(768, 512)
                d = dot(weights[:, dy * 768 : (dy + 1) * 768], a)
                v = d if v is None else v + d
            s = sigmoid(v)
            slope[p, :, cols] = (s * (1.0 + v * (1.0 - s))).astype(BF)
            u = v * s
            u = u[:128] + u[128:]
            total[:, cols] += u
        pltpu.make_async_copy(slope.at[p], slope_out.at[p], sems.at[p]).start()
        return carry

    total[...] = jnp.zeros_like(total)
    lax.fori_loop(0, 4, phase, 0)
    pooled[...] = (total[...] * 0.125).astype(BF)
    for p in range(4):
        pltpu.make_async_copy(slope.at[p], slope_out.at[p], sems.at[p]).wait()
    for c in saved:
        c.wait()


def fill_rows(parts, rows):
    for z, ref in enumerate(parts):
        for y in range(3):
            at = (z * 3 + y) * 128
            rows[at : at + 128, :] = shifted(ref[...], y - 1, 0)


def folded(weights, rows):
    y = [dot(weights[x * 128 : (x + 1) * 128, :], rows[...]) for x in range(3)]
    return y[1] + shifted(y[0], 0, -1) + shifted(y[2], 0, 1)


def second_body(
    core, lo, own, hi, got, act_mine, act_other, slopes, backward, rows, weights
):
    fold_taps(got, weights, backward)
    fill_rows([lo, own, hi], rows)
    v = folded(weights, rows)
    s = sigmoid(v)
    a = v * s
    g = s * (1.0 + v * (1.0 - s))
    for t in range(8):
        cols = slice(t * 128, (t + 1) * 128)
        cot = all_channels(got, slice(t * 8, (t + 1) * 8)).astype(F32)
        slopes[:, cols] = (cot * g[:, cols]).astype(BF)
        mine, other = by_core(core[0], a[:, cols].reshape(16, 8, 128))
        act_mine[:, t * 8 : (t + 1) * 8, :] = mine.astype(BF)
        act_other[:, t * 8 : (t + 1) * 8, :] = other.astype(BF)


def second_grad_body(core, lo, own, hi, slopes, act_mine, act_other, out_mine, out_other, planes):
    for y in range(3):
        for x in range(3):
            for z, ref in enumerate((lo, own, hi)):
                planes[y * 3 + x, z * 128 : (z + 1) * 128, :] = shifted(ref[...], y - 1, x - 1)
    for t in range(9):
        g = dot_nt(slopes[...], planes[t])
        for z in range(3):
            at = 64 + (z * 9 + t) * 8
            mine, other = by_core(core[0], g[:, z * 128 : (z + 1) * 128].reshape(16, 8, 128))
            out_mine[:, at : at + 8, :] = mine.astype(BF)
            out_other[:, at : at + 8, :] = other.astype(BF)
    out_mine[:, 0:64, :] = act_mine[...]
    out_other[:, 0:64, :] = act_other[...]


def share_of(row):
    return row // 112, row % 112


def put(core, parts, row, values):
    done = 0
    while done < 64:
        share, at = share_of(row + done)
        n = min(64 - done, 112 - at)
        side = jnp.where(core[0] == share % 2, 0, 1)
        parts[side, share // 2, at : at + n, :] = values[done : done + n].astype(BF)
        done += n


def first_grad_body(
    core, slo, own, shi, weights, slope_in, planes_in, first_slopes_out, out_mine, out_other, rows,
    windows, total, slope, planes, first_slopes, parts, sems,
):
    planes_copy = pltpu.make_async_copy(planes_in, planes, sems.at[5])
    planes_copy.start()
    slope_copy = pltpu.make_async_copy(slope_in, slope, sems.at[4])
    slope_copy.start()
    fill_rows([slo, own, shi], rows)
    ps = folded(weights, rows) * 0.125
    slope_copy.wait()
    for p in range(4):
        for z in range(2):
            first_slopes[p, z * 128 : (z + 1) * 128, :] = (
                ps * slope[p, z * 128 : (z + 1) * 128, :].astype(F32)
            ).astype(BF)
        pltpu.make_async_copy(first_slopes.at[p], first_slopes_out.at[p], sems.at[p]).start()
    planes_copy.wait()
    fill_windows([planes.at[k] for k in range(4)], windows)
    for dy in range(3):
        for p in range(4):
            py, px = p // 2, p % 2
            a = windows[(py + dy) * 4 + px : (py + dy) * 4 + px + 3].reshape(768, CELLS)
            d = dot_nt(a, first_slopes[p])
            if p == 0:
                total[...] = d
            else:
                total[...] += d
        for dx in range(3):
            for dz in range(3):
                t = dz * 9 + dy * 3 + dx
                at = dx * 256 + dz * 64
                g = total[at : at + 64, 0:128] + total[at + 64 : at + 128, 128:256]
                put(core, parts, t * 64, g)
    put(core, parts, 1728, jnp.zeros((64, 128), F32))
    out_mine[...] = parts[0]
    out_other[...] = parts[1]
    for p in range(4):
        pltpu.make_async_copy(first_slopes.at[p], first_slopes_out.at[p], sems.at[p]).wait()


def pair_body(core, b_mine, b_other, a_mine, a_other, out):
    c = core[0] == 0
    out[:, 0:64, :] = jnp.where(c, b_mine[:, 0:64, :].astype(F32), b_other[:, 0:64, :].astype(F32)).astype(BF)
    out[:, 64:128, :] = jnp.where(c, b_other[:, 0:64, :].astype(F32), b_mine[:, 0:64, :].astype(F32)).astype(BF)
    out[:, 128:240, :] = (a_mine[...].astype(F32) + a_other[...].astype(F32)).astype(BF)
    out[:, 240:456, :] = (b_mine[:, 64:280, :].astype(F32) + b_other[:, 64:280, :].astype(F32)).astype(BF)


def volume_grad_body(
    core, slopes_in, kin_in, own_out, near, far, windows, slopes, kin, weights, own, sems
):
    copies = [pltpu.make_async_copy(slopes_in.at[p], slopes.at[p], sems.at[p]) for p in range(4)]
    copies.append(pltpu.make_async_copy(kin_in, kin, sems.at[4]))
    for c in copies:
        c.start()
    for p in range(4):
        copies[p].wait()
        for iy, (py, oy) in enumerate(WINDOW):
            for ix, (px, ox) in enumerate(WINDOW):
                if py * 2 + px == p:
                    windows[iy * 4 + ix] = shifted(slopes[p], oy, ox)
    copies[4].wait()
    for t in range(9):
        weights[:, (8 - t) * 256 : (9 - t) * 256] = stacked_taps(kin, t)

    def phase(p, carry):
        py = p // 2
        px = p % 2
        for c in range(2):
            cols = slice(c * 512, (c + 1) * 512)
            v = None
            for dy in range(3):
                a = windows[pl.ds((py + dy) * 4 + px, 3), :, cols].reshape(768, 512)
                d = dot(weights[:, dy * 768 : (dy + 1) * 768], a)
                v = d if v is None else v + d
            at = pl.ds(pl.multiple_of(p * CELLS + c * 512, 512), 512)
            near[:, at] = jnp.where(core[0] == 0, v[192:256], v[0:64]).astype(BF)
            own[p, :, cols] = v[64:192]
            far[:, at] = jnp.where(core[0] == 0, v[0:64], v[192:256]).astype(BF)
        pltpu.make_async_copy(own.at[p], own_out.at[p], sems.at[5 + p]).start()
        return carry

    lax.fori_loop(0, 4, phase, 0)
    for p in range(4):
        pltpu.make_async_copy(own.at[p], own_out.at[p], sems.at[5 + p]).wait()


def join_body(core, own_in, near, far, out, tmp, own, sems):
    copies = []
    for h in range(2):
        for p in range(4):
            at = slice(h * 512, (h + 1) * 512)
            copies.append(
                pltpu.make_async_copy(own_in.at[p, :, at], own.at[p, :, at], sems.at[h * 4 + p])
            )
    for c in copies:
        c.start()
    pm = parity_matrix()
    for b in range(8):
        if b % 4 == 0:
            for c in copies[b : b + 4]:
                c.wait()
        pieces = []
        for p in range(4):
            at = slice(p * CELLS + b * 128, p * CELLS + (b + 1) * 128)
            lanes = slice(b * 128, (b + 1) * 128)
            n, f = near[:, at].astype(F32), far[:, at].astype(F32)
            first = own[p, 0:64, lanes] + jnp.where(core[0] == 0, f, n)
            second = own[p, 64:128, lanes] + jnp.where(core[0] == 0, n, f)
            pieces.append(jnp.concatenate([first, second], axis=0).astype(BF))
        y = dot_nt(jnp.concatenate(pieces, axis=1), pm)
        t = tmp.at[b % 2]
        for q in range(4):
            for z in range(2):
                t[q, pl.ds(z, 64, stride=2), :] = y[
                    z * 64 : (z + 1) * 64, q * 128 : (q + 1) * 128
                ]
        for q in range(4):
            at = slice(b * 512 + q * 128, b * 512 + (q + 1) * 128)
            out[0, :, :, at] = t[q].astype(BF).reshape(64, 2, 128)


def merge_body(got, out):
    y = jnp.sum(got[:, 128:456, :].astype(F32), axis=0).astype(BF)
    for k in range(4):
        out[k] = y


def row_sum_body(got, out):
    out[...] = jnp.sum(got[...].astype(F32), axis=0).astype(BF)


def unpack_body(got, act, tmp):
    for t in range(8):
        for side in range(2):
            at = side * 64 + t * 8
            tmp[side] = got[:, at : at + 8, :].astype(F32).reshape(64, 128)
        for o in range(8):
            planes = [tmp[side, pl.ds(o, 8, stride=8), :].reshape(8, 1, 128) for side in range(2)]
            both = jnp.concatenate(planes, axis=1).reshape(16, 128)
            act[0, o, :, t * 128 : (t + 1) * 128] = both.astype(BF)


def final_second_body(scale, a, b, out):
    y = (a[112:328, :].astype(F32) + b[112:328, :].astype(F32)) * scale
    for t in range(27):
        out[:, t * 128 : (t + 1) * 128] = y[t * 8 : (t + 1) * 8, :]


def final_first_body(scale, a, b, out):
    y = ((a[0:112, :].astype(F32) + b[0:112, :].astype(F32)) * scale).astype(BF)
    for k in range(8):
        out[k] = y


def widen_body(core, mine, other, out):
    for got, side in ((mine, core[0]), (other, 1 - core[0])):
        for q in range(7):
            row = pl.multiple_of((2 * q + side) * 112, 8)
            out[pl.ds(row, 112), :] = got[q].astype(F32)
        row = pl.multiple_of((14 + side) * 112, 8)
        out[pl.ds(row, 48), :] = got[7, 0:48, :].astype(F32)

        @pl.when(side == 0)
        def _():
            out[14 * 112 + 48 : 15 * 112, :] = got[7, 48:112, :].astype(F32)


def exchange(parts, axis):
    return lax.all_to_all(parts, axis, 0, 0, tiled=True)


def up(x):
    return lax.ppermute(x, SPACE, [(i, i + 1) for i in range(15)])


def down(x):
    return lax.ppermute(x, SPACE, [(i + 1, i) for i in range(15)])


def swap(x):
    return lax.ppermute(x, SPACE, [(i, i ^ 1) for i in range(16)])


def step(volume, kernel_in, kernel_out, cotangent):
    vm = pltpu.VMEM
    core = lax.axis_index("core").reshape(1)
    low, high = kernel_call(
        split_body, (shape((64, 4096)),) * 2, volume,
        scratch=[vm((2, 4, 128, 128), F32)], mib=8,
    )
    lo, hi = up(high), down(low)
    packed = kernel_call(
        send_body, shape((16, 280, 128)), cotangent, kernel_out.T,
        scratch=[
            vm((2, 128, 128), F32), vm((1, 8, 16, CELLS), BF), vm((8, 3456), BF),
            pltpu.SemaphoreType.DMA((2,)),
        ],
        mib=8, hbm_in=(0, 1),
    )
    got = exchange(packed, SPACE)
    w1 = kernel_call(first_weights_body, shape((256, 2304)), kernel_in, mib=8)
    pooled, slope, planes = kernel_call(
        first_body,
        (shape((128, CELLS)), shape((4, 256, CELLS)), shape((4, 64, 4096))), lo, low, high, hi, w1,
        scratch=[
            vm((16, 256, CELLS), BF), vm((128, CELLS), F32), vm((4, 256, CELLS), BF),
            pltpu.SemaphoreType.DMA((8,)),
        ],
        mib=20, hbm_out=(1, 2),
    )
    plo, phi = up(pooled), down(pooled)
    act_mine, act_other, slopes, w2b = kernel_call(
        second_body,
        (shape((8, 64, 128)), shape((8, 64, 128)), shape((128, CELLS)), shape((384, 1152))),
        core, plo, pooled, phi, got, scratch=[vm((1152, CELLS), BF), vm((384, 1152), BF)],
        mib=14, scalar=(0,),
    )
    slo, shi = up(slopes), down(slopes)
    b_mine, b_other = kernel_call(
        second_grad_body, (shape((8, 280, 128)),) * 2,
        core, plo, pooled, phi, slopes, act_mine, act_other,
        scratch=[vm((9, 384, CELLS), BF)], mib=14, scalar=(0,),
    )
    b_other = swap(b_other)
    first_slopes, a_mine, a_other = kernel_call(
        first_grad_body,
        (shape((4, 256, CELLS)), shape((8, 112, 128)), shape((8, 112, 128))),
        core, slo, slopes, shi, w2b, slope, planes,
        scratch=[
            vm((1152, CELLS), BF), vm((16, 256, CELLS), BF), vm((768, 256), F32),
            vm((4, 256, CELLS), BF), vm((4, 64, 4096), BF), vm((4, 256, CELLS), BF),
            vm((2, 8, 112, 128), BF), pltpu.SemaphoreType.DMA((6,)),
        ],
        mib=28, scalar=(0,), hbm_in=(5, 6), hbm_out=(0,),
    )
    a_other = swap(a_other)
    packed = kernel_call(
        pair_body, shape((8, 456, 128)), core, b_mine, b_other, a_mine, a_other,
        mib=8, scalar=(0,),
    )
    got = exchange(packed, "chip")
    own, near, far = kernel_call(
        volume_grad_body, (shape((4, 128, CELLS), F32), shape((64, 4096)), shape((64, 4096))),
        core, first_slopes, kernel_in,
        scratch=[
            vm((16, 256, CELLS), BF), vm((4, 256, CELLS), BF), vm((1728, 128), BF),
            vm((256, 2304), BF), vm((4, 128, CELLS), F32), pltpu.SemaphoreType.DMA((9,)),
        ],
        mib=24, scalar=(0,), hbm_in=(1, 2), hbm_out=(0,),
    )
    near = swap(near)
    pairs = [(i, i + 1) for i in range(1, 14, 2)]
    far = lax.ppermute(far, SPACE, pairs + [(b, a) for a, b in pairs])
    packed = kernel_call(merge_body, shape((4, 328, 128)), got, mib=8)
    rows = exchange(packed, "x")
    row = kernel_call(row_sum_body, shape((328, 128)), rows, mib=8)
    row_far = lax.ppermute(row, "zh", [(0, 1), (1, 0)])
    activation = kernel_call(
        unpack_body, shape((1, 8, 16, CELLS)), got, scratch=[vm((2, 64, 128), F32)],
        mib=8,
    )
    cell_count = 8 * 32 * 4096
    packed = kernel_call(
        lambda a, b, o: final_first_body(1.0 / math.sqrt(cell_count), a, b, o),
        shape((8, 112, 128)), row, row_far, mib=8,
    )
    got = exchange(packed, "chip")
    got_other = swap(got)
    volume_grad = kernel_call(
        join_body, shape((1, 64, 2, 4096)), core, own, near, far,
        scratch=[vm((2, 4, 128, 128), F32), vm((4, 128, CELLS), F32), pltpu.SemaphoreType.DMA((8,))],
        mib=12, scalar=(0,), hbm_in=(1,),
    )
    second_grad = kernel_call(
        lambda a, b, o: final_second_body(1.0 / math.sqrt(cell_count // 8), a, b, o),
        shape((8, 3456), F32), row, row_far, mib=8,
    ).T
    first_grad = kernel_call(
        widen_body, shape((1728, 128), F32), core, got, got_other, mib=8, scalar=(0,)
    )
    return activation, volume_grad, first_grad, second_grad


def solution(mesh):
    finer = Mesh(mesh.devices.reshape(2, 4, 8, 2), ("zh", "x", "chip", "core"))
    return jax.shard_map(
        step,
        mesh=finer,
        in_specs=(P(DP, None, SPACE, None), P(), P(None, SPACE), P(DP, SPACE, None, None)),
        out_specs=(P(DP, SPACE, None, None), P(DP, None, SPACE, None), P(), P(None, SPACE)),
        check_vma=False,
    )
```

```python
import math

import jax
import jax.numpy as jnp
from jax import lax
from jax.experimental import pallas as pl
from jax.experimental.pallas import tpu as pltpu
from jax.sharding import Mesh
from jax.sharding import PartitionSpec as P


BF = jnp.bfloat16
F32 = jnp.float32
WINDOW = ((1, -1), (0, 0), (1, 0), (0, 1))
CELLS = 1024
NT = (((1,), (1,)), ((), ()))
DP = ("zh", "x")
SPACE = ("chip", "core")


def shape(dims, kind=BF):
    return jax.ShapeDtypeStruct(dims, kind)


def kernel_call(body, outs, *args, scratch=(), mib, hbm_in=(), hbm_out=(), scalar=()):
    def spec(k, far):
        if k in far:
            return pl.BlockSpec(memory_space=pltpu.HBM)
        return pl.BlockSpec()

    ins = [
        pl.BlockSpec(memory_space=pltpu.SMEM) if k in scalar else spec(k, hbm_in)
        for k in range(len(args))
    ]
    args = [
        pltpu.with_memory_space_constraint(x, pltpu.HBM) if k in hbm_in else x
        for k, x in enumerate(args)
    ]
    many = isinstance(outs, tuple)
    listed = outs if many else (outs,)
    out_specs = tuple(spec(k, hbm_out) for k in range(len(listed)))
    placed = tuple(
        pltpu.HBM(o.shape, o.dtype) if k in hbm_out else o for k, o in enumerate(listed)
    )
    return pl.pallas_call(
        body,
        out_shape=placed if many else placed[0],
        in_specs=ins,
        out_specs=out_specs if many else out_specs[0],
        scratch_shapes=list(scratch),
        compiler_params=pltpu.CompilerParams(vmem_limit_bytes=mib << 20),
    )(*args)


def dot(a, b):
    return jnp.dot(a, b, preferred_element_type=F32)


def dot_nt(a, b):
    return lax.dot_general(a, b, NT, preferred_element_type=F32)


def sigmoid(v):
    return 1.0 / (1.0 + jnp.exp(-v))


def parity_matrix():
    row = lax.broadcasted_iota(jnp.int32, (512, 512), 0)
    col = lax.broadcasted_iota(jnp.int32, (512, 512), 1)
    phase = col // 128
    source = (2 * ((col % 128) // 32) + phase // 2) * 64 + 2 * (col % 32) + phase % 2
    return (row == source).astype(F32).astype(BF)


def shifted(x, oy, ox):
    step = (-(oy * 32 + ox)) % CELLS
    y = pltpu.roll(x, step, 1) if step else x
    if not (oy or ox):
        return y
    lane = lax.broadcasted_iota(jnp.int32, (1, CELLS), 1)
    keep = None
    if oy:
        keep = lane < CELLS - 32 if oy == 1 else lane >= 32
    if ox:
        inside = (lane % 32) != (31 if ox == 1 else 0)
        keep = inside if keep is None else keep & inside
    return jnp.where(keep, y, jnp.zeros((), x.dtype))


def fill_windows(parts, windows):
    for iy, (py, oy) in enumerate(WINDOW):
        for ix, (px, ox) in enumerate(WINDOW):
            at = (py * 2 + px) * CELLS
            for k, ref in parts:
                row = k * 64 if isinstance(k, int) else pl.multiple_of(k * 64, 64)
                windows[iy * 4 + ix, pl.ds(row, 64), :] = shifted(ref[:, at : at + CELLS], oy, ox)


def split_body(core, vol, near, far, tmp):
    pm = parity_matrix()
    for b in range(8):
        y = dot(vol[0, :, :, b * 512 : (b + 1) * 512].reshape(128, 512), pm)
        t = tmp.at[b % 2]
        for p in range(4):
            t[p] = y[:, p * 128 : (p + 1) * 128]
        for z, out in ((1 - core[0], near), (core[0], far)):
            for p in range(4):
                out[:, p * CELLS + b * 128 : p * CELLS + (b + 1) * 128] = t[
                    p, pl.ds(z, 64, stride=2), :
                ].astype(BF)


def stacked_taps(kin, t):
    zero = jnp.zeros((64, 128), BF)

    def block(dz):
        return kin[(dz * 9 + t) * 64 : (dz * 9 + t + 1) * 64, :] if 0 <= dz <= 2 else zero

    rows = [jnp.concatenate([block(z), block(z - 1)], axis=1) for z in range(4)]
    return jnp.concatenate(rows, axis=0)


def first_weights_body(kin_in, out, kin, weights, sems):
    copy = pltpu.make_async_copy(kin_in, kin, sems.at[0])
    copy.start()
    copy.wait()
    for t in range(9):
        weights[:, t * 256 : (t + 1) * 256] = stacked_taps(kin, t).T
    copy = pltpu.make_async_copy(weights, out, sems.at[1])
    copy.start()
    copy.wait()


def send_body(cot_in, kout_in, out, tmp, cot, kout, sems):
    copies = [
        pltpu.make_async_copy(cot_in, cot, sems.at[0]),
        pltpu.make_async_copy(kout_in, kout, sems.at[1]),
    ]
    for c in copies:
        c.start()
    copies[0].wait()
    for t in range(8):
        tmp[t % 2] = cot[0, :, :, t * 128 : (t + 1) * 128].astype(F32).reshape(128, 128)
        for z in range(16):
            out[z, t * 8 : (t + 1) * 8, :] = tmp[t % 2, pl.ds(z, 8, stride=16), :].astype(BF)
    copies[1].wait()
    for t in range(27):
        block = kout[:, t * 128 : (t + 1) * 128]
        for z in range(16):
            out[z, 64 + t * 8 : 72 + t * 8, :] = block


def all_channels(got, at):
    return got[:, at, :].reshape(128, 128)


def fold_taps(got, forward, backward):
    for t in range(27):
        z, y, x = t // 9, (t // 3) % 3, t % 3
        block = all_channels(got, slice(64 + t * 8, 72 + t * 8))
        forward[x * 128 : (x + 1) * 128, (z * 3 + y) * 128 : (z * 3 + y + 1) * 128] = block
        z, y, x = 2 - z, 2 - y, 2 - x
        backward[x * 128 : (x + 1) * 128, (z * 3 + y) * 128 : (z * 3 + y + 1) * 128] = block.T


def by_core(core, x):
    x = x.reshape(8, 2, *x.shape[1:])
    even, odd = x[:, 0], x[:, 1]
    return jnp.where(core == 0, even, odd), jnp.where(core == 0, odd, even)


def first_body(
    core, near, far, got_near, got_far, weights_in, pooled, slope_out, planes_out, windows, total,
    slope, weights, sems,
):
    inner = jnp.where(core[0] == 0, 2, 1)
    outer = jnp.where(core[0] == 0, 3, 0)
    parts = [(inner, near), (3 - inner, far), (outer, got_near), (3 - outer, got_far)]
    weights_copy = pltpu.make_async_copy(weights_in, weights, sems.at[8])
    weights_copy.start()
    saved = [
        pltpu.make_async_copy(r, planes_out.at[k], sems.at[4 + n]) for n, (k, r) in enumerate(parts)
    ]
    for c in saved:
        c.start()
    fill_windows(parts, windows)
    weights_copy.wait()

    def phase(p, carry):
        py = p // 2
        px = p % 2
        for c in range(2):
            cols = slice(c * 512, (c + 1) * 512)
            v = None
            for dy in range(3):
                a = windows[pl.ds((py + dy) * 4 + px, 3), :, cols].reshape(768, 512)
                d = dot(weights[:, dy * 768 : (dy + 1) * 768], a)
                v = d if v is None else v + d
            s = sigmoid(v)
            slope[p, :, cols] = (s * (1.0 + v * (1.0 - s))).astype(BF)
            u = v * s
            u = u[:128] + u[128:]
            total[:, cols] += u
        pltpu.make_async_copy(slope.at[p], slope_out.at[p], sems.at[p]).start()
        return carry

    total[...] = jnp.zeros_like(total)
    lax.fori_loop(0, 4, phase, 0)
    pooled[...] = (total[...] * 0.125).astype(BF)
    for p in range(4):
        pltpu.make_async_copy(slope.at[p], slope_out.at[p], sems.at[p]).wait()
    for c in saved:
        c.wait()


def fill_rows(parts, rows):
    for z, ref in enumerate(parts):
        for y in range(3):
            at = (z * 3 + y) * 128
            rows[at : at + 128, :] = shifted(ref[...], y - 1, 0)


def folded(weights, rows):
    y = [dot(weights[x * 128 : (x + 1) * 128, :], rows[...]) for x in range(3)]
    return y[1] + shifted(y[0], 0, -1) + shifted(y[2], 0, 1)


def second_body(
    core, lo, own, hi, got, act_mine, act_other, slopes, backward, rows, weights
):
    fold_taps(got, weights, backward)
    fill_rows([lo, own, hi], rows)
    v = folded(weights, rows)
    s = sigmoid(v)
    a = v * s
    g = s * (1.0 + v * (1.0 - s))
    for t in range(8):
        cols = slice(t * 128, (t + 1) * 128)
        cot = all_channels(got, slice(t * 8, (t + 1) * 8)).astype(F32)
        slopes[:, cols] = (cot * g[:, cols]).astype(BF)
        mine, other = by_core(core[0], a[:, cols].reshape(16, 8, 128))
        act_mine[:, t * 8 : (t + 1) * 8, :] = mine.astype(BF)
        act_other[:, t * 8 : (t + 1) * 8, :] = other.astype(BF)


def second_grad_body(core, lo, own, hi, slopes, act_mine, act_other, out_mine, out_other, planes):
    for y in range(3):
        for x in range(3):
            for z, ref in enumerate((lo, own, hi)):
                planes[y * 3 + x, z * 128 : (z + 1) * 128, :] = shifted(ref[...], y - 1, x - 1)
    for t in range(9):
        g = dot_nt(slopes[...], planes[t])
        for z in range(3):
            at = 64 + (z * 9 + t) * 8
            mine, other = by_core(core[0], g[:, z * 128 : (z + 1) * 128].reshape(16, 8, 128))
            out_mine[:, at : at + 8, :] = mine.astype(BF)
            out_other[:, at : at + 8, :] = other.astype(BF)
    out_mine[:, 0:64, :] = act_mine[...]
    out_other[:, 0:64, :] = act_other[...]


def share_of(row):
    return row // 112, row % 112


def put(core, parts, row, values):
    done = 0
    while done < 64:
        share, at = share_of(row + done)
        n = min(64 - done, 112 - at)
        side = jnp.where(core[0] == share % 2, 0, 1)
        parts[side, share // 2, at : at + n, :] = values[done : done + n].astype(BF)
        done += n


def first_grad_body(
    core, slo, own, shi, weights, slope_in, planes_in, first_slopes_out, out_mine, out_other, rows,
    windows, total, slope, planes, first_slopes, parts, sems,
):
    planes_copy = pltpu.make_async_copy(planes_in, planes, sems.at[5])
    planes_copy.start()
    slope_copy = pltpu.make_async_copy(slope_in, slope, sems.at[4])
    slope_copy.start()
    fill_rows([slo, own, shi], rows)
    ps = folded(weights, rows) * 0.125
    slope_copy.wait()
    for p in range(4):
        for z in range(2):
            first_slopes[p, z * 128 : (z + 1) * 128, :] = (
                ps * slope[p, z * 128 : (z + 1) * 128, :].astype(F32)
            ).astype(BF)
        pltpu.make_async_copy(first_slopes.at[p], first_slopes_out.at[p], sems.at[p]).start()
    planes_copy.wait()
    fill_windows([(k, planes.at[k]) for k in range(4)], windows)
    for dy in range(3):
        for p in range(4):
            py, px = p // 2, p % 2
            a = windows[(py + dy) * 4 + px : (py + dy) * 4 + px + 3].reshape(768, CELLS)
            d = dot_nt(a, first_slopes[p])
            if p == 0:
                total[...] = d
            else:
                total[...] += d
        for dx in range(3):
            for dz in range(3):
                t = dz * 9 + dy * 3 + dx
                at = dx * 256 + dz * 64
                g = total[at : at + 64, 0:128] + total[at + 64 : at + 128, 128:256]
                put(core, parts, t * 64, g)
    put(core, parts, 1728, jnp.zeros((64, 128), F32))
    out_mine[...] = parts[0]
    out_other[...] = parts[1]
    for p in range(4):
        pltpu.make_async_copy(first_slopes.at[p], first_slopes_out.at[p], sems.at[p]).wait()


def pair_body(core, b_mine, b_other, a_mine, a_other, out):
    c = core[0] == 0
    out[:, 0:64, :] = jnp.where(c, b_mine[:, 0:64, :].astype(F32), b_other[:, 0:64, :].astype(F32)).astype(BF)
    out[:, 64:128, :] = jnp.where(c, b_other[:, 0:64, :].astype(F32), b_mine[:, 0:64, :].astype(F32)).astype(BF)
    out[:, 128:240, :] = (a_mine[...].astype(F32) + a_other[...].astype(F32)).astype(BF)
    out[:, 240:456, :] = (b_mine[:, 64:280, :].astype(F32) + b_other[:, 64:280, :].astype(F32)).astype(BF)


def volume_grad_body(
    core, slopes_in, kin_in, own_out, near, far, windows, slopes, kin, weights, own, sems
):
    copies = [pltpu.make_async_copy(slopes_in.at[p], slopes.at[p], sems.at[p]) for p in range(4)]
    copies.append(pltpu.make_async_copy(kin_in, kin, sems.at[4]))
    for c in copies:
        c.start()
    for p in range(4):
        copies[p].wait()
        for iy, (py, oy) in enumerate(WINDOW):
            for ix, (px, ox) in enumerate(WINDOW):
                if py * 2 + px == p:
                    windows[iy * 4 + ix] = shifted(slopes[p], oy, ox)
    copies[4].wait()
    for t in range(9):
        weights[:, (8 - t) * 256 : (9 - t) * 256] = stacked_taps(kin, t)

    def phase(p, carry):
        py = p // 2
        px = p % 2
        for c in range(2):
            cols = slice(c * 512, (c + 1) * 512)
            v = None
            for dy in range(3):
                a = windows[pl.ds((py + dy) * 4 + px, 3), :, cols].reshape(768, 512)
                d = dot(weights[:, dy * 768 : (dy + 1) * 768], a)
                v = d if v is None else v + d
            at = pl.ds(pl.multiple_of(p * CELLS + c * 512, 512), 512)
            near[:, at] = jnp.where(core[0] == 0, v[192:256], v[0:64]).astype(BF)
            own[p, :, cols] = v[64:192]
            far[:, at] = jnp.where(core[0] == 0, v[0:64], v[192:256]).astype(BF)
        pltpu.make_async_copy(own.at[p], own_out.at[p], sems.at[5 + p]).start()
        return carry

    lax.fori_loop(0, 4, phase, 0)
    for p in range(4):
        pltpu.make_async_copy(own.at[p], own_out.at[p], sems.at[5 + p]).wait()


def join_body(core, own_in, near, far, out, tmp, own, sems):
    copies = []
    for h in range(2):
        for p in range(4):
            at = slice(h * 512, (h + 1) * 512)
            copies.append(
                pltpu.make_async_copy(own_in.at[p, :, at], own.at[p, :, at], sems.at[h * 4 + p])
            )
    for c in copies:
        c.start()
    pm = parity_matrix()
    for b in range(8):
        if b % 4 == 0:
            for c in copies[b : b + 4]:
                c.wait()
        pieces = []
        for p in range(4):
            at = slice(p * CELLS + b * 128, p * CELLS + (b + 1) * 128)
            lanes = slice(b * 128, (b + 1) * 128)
            n, f = near[:, at].astype(F32), far[:, at].astype(F32)
            first = own[p, 0:64, lanes] + jnp.where(core[0] == 0, f, n)
            second = own[p, 64:128, lanes] + jnp.where(core[0] == 0, n, f)
            pieces.append(jnp.concatenate([first, second], axis=0).astype(BF))
        y = dot_nt(jnp.concatenate(pieces, axis=1), pm)
        t = tmp.at[b % 2]
        for q in range(4):
            for z in range(2):
                t[q, pl.ds(z, 64, stride=2), :] = y[
                    z * 64 : (z + 1) * 64, q * 128 : (q + 1) * 128
                ]
        for q in range(4):
            at = slice(b * 512 + q * 128, b * 512 + (q + 1) * 128)
            out[0, :, :, at] = t[q].astype(BF).reshape(64, 2, 128)


def merge_body(got, out):
    y = jnp.sum(got[:, 128:456, :].astype(F32), axis=0).astype(BF)
    for k in range(4):
        out[k] = y


def row_sum_body(got, out):
    out[...] = jnp.sum(got[...].astype(F32), axis=0).astype(BF)


def unpack_body(got, act, tmp):
    for t in range(8):
        for side in range(2):
            at = side * 64 + t * 8
            tmp[side] = got[:, at : at + 8, :].astype(F32).reshape(64, 128)
        for o in range(8):
            planes = [tmp[side, pl.ds(o, 8, stride=8), :].reshape(8, 1, 128) for side in range(2)]
            both = jnp.concatenate(planes, axis=1).reshape(16, 128)
            act[0, o, :, t * 128 : (t + 1) * 128] = both.astype(BF)


def final_second_body(scale, a, b, out):
    y = (a[112:328, :].astype(F32) + b[112:328, :].astype(F32)) * scale
    for t in range(27):
        out[:, t * 128 : (t + 1) * 128] = y[t * 8 : (t + 1) * 8, :]


def final_first_body(scale, a, b, out):
    y = ((a[0:112, :].astype(F32) + b[0:112, :].astype(F32)) * scale).astype(BF)
    for k in range(8):
        out[k] = y


def widen_body(core, mine, other, out):
    for got, side in ((mine, core[0]), (other, 1 - core[0])):
        for q in range(7):
            row = pl.multiple_of((2 * q + side) * 112, 8)
            out[pl.ds(row, 112), :] = got[q].astype(F32)
        row = pl.multiple_of((14 + side) * 112, 8)
        out[pl.ds(row, 48), :] = got[7, 0:48, :].astype(F32)

        @pl.when(side == 0)
        def _():
            out[14 * 112 + 48 : 15 * 112, :] = got[7, 48:112, :].astype(F32)


def exchange(parts, axis):
    return lax.all_to_all(parts, axis, 0, 0, tiled=True)


def up(x):
    return lax.ppermute(x, SPACE, [(i, i + 1) for i in range(15)])


def down(x):
    return lax.ppermute(x, SPACE, [(i + 1, i) for i in range(15)])


def swap(x):
    return lax.ppermute(x, SPACE, [(i, i ^ 1) for i in range(16)])


def across(x):
    pairs = [(i, i + 1) for i in range(1, 14, 2)]
    return lax.ppermute(x, SPACE, pairs + [(b, a) for a, b in pairs])


def step(volume, kernel_in, kernel_out, cotangent):
    vm = pltpu.VMEM
    core = lax.axis_index("core").reshape(1)
    near, far = kernel_call(
        split_body, (shape((64, 4096)),) * 2, core, volume, scratch=[vm((2, 4, 128, 128), F32)],
        mib=8, scalar=(0,),
    )
    got_far, got_near = across(far), swap(near)
    packed = kernel_call(
        send_body, shape((16, 280, 128)), cotangent, kernel_out.T,
        scratch=[
            vm((2, 128, 128), F32), vm((1, 8, 16, CELLS), BF), vm((8, 3456), BF),
            pltpu.SemaphoreType.DMA((2,)),
        ],
        mib=8, hbm_in=(0, 1),
    )
    got = exchange(packed, SPACE)
    w1 = kernel_call(
        first_weights_body, shape((256, 2304)), kernel_in,
        scratch=[vm((1728, 128), BF), vm((256, 2304), BF), pltpu.SemaphoreType.DMA((2,))],
        mib=8, hbm_in=(0,), hbm_out=(0,),
    )
    pooled, slope, planes = kernel_call(
        first_body,
        (shape((128, CELLS)), shape((4, 256, CELLS)), shape((4, 64, 4096))),
        core, near, far, got_near, got_far, w1,
        scratch=[
            vm((16, 256, CELLS), BF), vm((128, CELLS), F32), vm((4, 256, CELLS), BF),
            vm((256, 2304), BF), pltpu.SemaphoreType.DMA((9,)),
        ],
        mib=22, scalar=(0,), hbm_in=(5,), hbm_out=(1, 2),
    )
    plo, phi = up(pooled), down(pooled)
    act_mine, act_other, slopes, w2b = kernel_call(
        second_body,
        (shape((8, 64, 128)), shape((8, 64, 128)), shape((128, CELLS)), shape((384, 1152))),
        core, plo, pooled, phi, got, scratch=[vm((1152, CELLS), BF), vm((384, 1152), BF)],
        mib=14, scalar=(0,),
    )
    slo, shi = up(slopes), down(slopes)
    b_mine, b_other = kernel_call(
        second_grad_body, (shape((8, 280, 128)),) * 2,
        core, plo, pooled, phi, slopes, act_mine, act_other,
        scratch=[vm((9, 384, CELLS), BF)], mib=14, scalar=(0,),
    )
    b_other = swap(b_other)
    first_slopes, a_mine, a_other = kernel_call(
        first_grad_body,
        (shape((4, 256, CELLS)), shape((8, 112, 128)), shape((8, 112, 128))),
        core, slo, slopes, shi, w2b, slope, planes,
        scratch=[
            vm((1152, CELLS), BF), vm((16, 256, CELLS), BF), vm((768, 256), F32),
            vm((4, 256, CELLS), BF), vm((4, 64, 4096), BF), vm((4, 256, CELLS), BF),
            vm((2, 8, 112, 128), BF), pltpu.SemaphoreType.DMA((6,)),
        ],
        mib=28, scalar=(0,), hbm_in=(5, 6), hbm_out=(0,),
    )
    a_other = swap(a_other)
    packed = kernel_call(
        pair_body, shape((8, 456, 128)), core, b_mine, b_other, a_mine, a_other,
        mib=8, scalar=(0,),
    )
    got = exchange(packed, "chip")
    own, near, far = kernel_call(
        volume_grad_body, (shape((4, 128, CELLS), F32), shape((64, 4096)), shape((64, 4096))),
        core, first_slopes, kernel_in,
        scratch=[
            vm((16, 256, CELLS), BF), vm((4, 256, CELLS), BF), vm((1728, 128), BF),
            vm((256, 2304), BF), vm((4, 128, CELLS), F32), pltpu.SemaphoreType.DMA((9,)),
        ],
        mib=24, scalar=(0,), hbm_in=(1, 2), hbm_out=(0,),
    )
    near = swap(near)
    far = across(far)
    packed = kernel_call(merge_body, shape((4, 328, 128)), got, mib=8)
    rows = exchange(packed, "x")
    row = kernel_call(row_sum_body, shape((328, 128)), rows, mib=8)
    row_far = lax.ppermute(row, "zh", [(0, 1), (1, 0)])
    activation = kernel_call(
        unpack_body, shape((1, 8, 16, CELLS)), got, scratch=[vm((2, 64, 128), F32)],
        mib=8,
    )
    cell_count = 8 * 32 * 4096
    packed = kernel_call(
        lambda a, b, o: final_first_body(1.0 / math.sqrt(cell_count), a, b, o),
        shape((8, 112, 128)), row, row_far, mib=8,
    )
    got = exchange(packed, "chip")
    got_other = swap(got)
    volume_grad = kernel_call(
        join_body, shape((1, 64, 2, 4096)), core, own, near, far,
        scratch=[vm((2, 4, 128, 128), F32), vm((4, 128, CELLS), F32), pltpu.SemaphoreType.DMA((8,))],
        mib=12, scalar=(0,), hbm_in=(1,),
    )
    second_grad = kernel_call(
        lambda a, b, o: final_second_body(1.0 / math.sqrt(cell_count // 8), a, b, o),
        shape((8, 3456), F32), row, row_far, mib=8,
    ).T
    first_grad = kernel_call(
        widen_body, shape((1728, 128), F32), core, got, got_other, mib=8, scalar=(0,)
    )
    return activation, volume_grad, first_grad, second_grad


def solution(mesh):
    finer = Mesh(mesh.devices.reshape(2, 4, 8, 2), ("zh", "x", "chip", "core"))
    return jax.shard_map(
        step,
        mesh=finer,
        in_specs=(P(DP, None, SPACE, None), P(), P(None, SPACE), P(DP, SPACE, None, None)),
        out_specs=(P(DP, SPACE, None, None), P(DP, None, SPACE, None), P(), P(None, SPACE)),
        check_vma=False,
    )
```
